128 devices in a mesh: lon: 64 (over z, x, y), lev: 2 (over core).
Axes of the slice: x: 4, y: 4, z: 4, core: 2. Of those that a mesh axis runs over, the one named last changes fastest.
Arguments:
- ensemble: float32 [80, 16, 65536], P(None, 'lev', 'lon'), may hold values from -6 to 6
- obs_cell: int32 [12, 128], P(None, 'lon'), may hold values from 0 to 65535, as said below
- obs_value: float32 [12, 128], P(None, 'lon'), may hold values from -5 to 5
- obs_noise: float32 [12, 128], P(None, 'lon'), may hold values from 0.2 to 2
- obs_weight: float32 [12, 16, 128], P(None, 'lev'), may hold values from 0.05 to 0.5
- tile_lists: int32 [12, 1536], P(None, 'lon'), may hold values from 0 to 128, as said below
- batch_order: int32 [12], replicated, may hold values from 0 to 11, each once
Outputs:
- analysis: float32 [80, 16, 65536], P(None, 'lev', 'lon')
The draws below stay inside these ranges and needn't reach their ends.
Inputs may be any that keep to these rules, and one draw needn't show every extreme that they name: `obs_cell`: each tile holds at most 8 observations of one block, and some tile exactly 8. `tile_lists`: for block b and tile t the tile's 24 slots hold first, ascending and once each, the observations of block b whose tile is t or a neighbour of t around the globe, then the value 128 in every remaining slot; in every block some tile has all 24 slots used. `batch_order`: each block once.
All inputs are finite; a program needn't handle non-finite values.
Results may differ from the reference program's by a relative error of at most 0.0003.
Values sent between devices are 32-bit elements; how exact they have to be, the bound alone decides.
No kernel may reach another device: no remote copies, remote signals or barrier semaphores. Data moves between devices by JAX's collectives and lax.ppermute only.
A program may use at most 128 MiB of HBM per device.

```python
import math
import jax
import jax.numpy as jnp
from jax import lax

MEM = 80
OBS = 128
OWN_MAX = 8
ROUTE_CAP = 24
LON_DEV = 16
CELL_DEV = 1024
BATCHES = 12
LEVELS = 16
CELLS = 65536
N_LON = 64


def block_layout(key):
    subkeys = jax.random.split(jax.random.fold_in(key, 7351), BATCHES)

    def single(subkey):
        pick_key = jax.random.fold_in(subkey, 0)
        order_key = jax.random.fold_in(subkey, 1)
        cell_key = jax.random.fold_in(subkey, 2)
        shuffle_key = jax.random.fold_in(subkey, 4)
        slot_count = N_LON * OWN_MAX
        slot_tile = jnp.arange(slot_count, dtype=jnp.int32) // OWN_MAX
        centre = jax.random.randint(pick_key, (), 0, N_LON)
        forward = (slot_tile - centre) % N_LON
        backward = (centre - slot_tile) % N_LON
        nearby = (jnp.minimum(forward, backward) <= 1).astype(jnp.int32)
        score = jax.random.permutation(order_key, slot_count).astype(jnp.int32) + nearby * slot_count
        chosen = lax.top_k(score, OBS)[1].astype(jnp.int32)
        chosen = jax.random.permutation(shuffle_key, chosen)
        tiles = slot_tile[chosen]
        cell_ids = tiles * CELL_DEV + jax.random.randint(cell_key, (OBS,), 0, CELL_DEV)
        tile_ids = jnp.arange(N_LON, dtype=jnp.int32)
        distance_tiles = (tiles[None, :] - tile_ids[:, None]) % N_LON
        reached = (distance_tiles <= 1) | (distance_tiles == N_LON - 1)
        total = jnp.sum(reached.astype(jnp.int32), axis=1)
        numbers = jnp.arange(OBS, dtype=jnp.int32)
        ordering = jnp.where(reached, numbers[None, :], numbers[None, :] + OBS)
        ordered = jnp.argsort(ordering, axis=1, stable=True)[:, :ROUTE_CAP].astype(jnp.int32)
        slot_ids = jnp.arange(ROUTE_CAP, dtype=jnp.int32)
        lists = jnp.where(slot_ids[None, :] < total[:, None], ordered, OBS)
        return (cell_ids, lists.reshape(-1).astype(jnp.int32))
    return jax.vmap(single)(subkeys)


def draw_obs_cell(key, part):
    return block_layout(key)[0]


def draw_tile_lists(key, part):
    return block_layout(key)[1]


def shard_levels(stream_key, shape, cuts, least, top_value):
    gain, own = 1.0, jax.random.fold_in(stream_key, 6)
    for axis_at, parts in cuts:
        draws = jnp.exp(jax.random.uniform(jax.random.fold_in(own, axis_at), (parts,), jnp.float32, least / len(cuts), top_value / len(cuts)))
        gain = gain * jnp.repeat(draws, shape[axis_at] // parts).reshape([-1 if axis == axis_at else 1 for axis in range(len(shape))])
    return gain


def normal_values(key, extent, scale, limit, shards=(), held_as=jnp.bfloat16):
    entries = jax.random.normal(key, extent, jnp.float32) * scale
    if len(shards) > 0:
        entries = shard_levels(key, extent, shards, -0.22, 0.18) * entries
    return jnp.clip(entries, min=-limit, max=limit).astype(held_as)


def setup_inputs(seed: int = 0) -> dict:
    streams_of = jax.random.split(jax.random.key(seed), 8)
    return {
        "ensemble": normal_values(streams_of[0], (MEM, LEVELS, CELLS), 1.0, 6.0, ((1, 2), (2, 64)), jnp.float32),
        "obs_cell": draw_obs_cell(jax.random.fold_in(streams_of[7], 71), 0),
        "obs_value": normal_values(streams_of[2], (BATCHES, OBS), 1.0, 5.0, ((1, 64),), jnp.float32),
        "obs_noise": jnp.clip(jnp.exp(math.log(2.0) - 2.3025851 * jax.random.uniform(streams_of[3], (BATCHES, OBS), jnp.float32) ** shard_levels(streams_of[3], (BATCHES, OBS), ((1, 64),), -0.2, 0.2)), 0.2, 2.0),
        "obs_weight": jnp.clip(jnp.exp(math.log(0.5) - 2.3025851 * jax.random.uniform(streams_of[4], (BATCHES, LEVELS, OBS), jnp.float32) ** shard_levels(streams_of[4], (BATCHES, LEVELS, OBS), ((1, 2),), -0.2, 0.2)), 0.05, 0.5),
        "tile_lists": draw_tile_lists(jax.random.fold_in(streams_of[7], 71), 0),
        "batch_order": jax.random.permutation(streams_of[6], BATCHES).astype(jnp.int32),
    }


highest = lax.Precision.HIGHEST

def locate(cell_ids):
    within = cell_ids % CELL_DEV
    return (within // LON_DEV, cell_ids // CELL_DEV * LON_DEV + within % LON_DEV)

def taper_weight(source_ids, target_ids, circle):
    source_row, source_col = locate(source_ids)
    target_row, target_col = locate(target_ids)
    apart_cols = jnp.abs(source_col[:, None] - target_col[None, :])
    apart_cols = jnp.minimum(apart_cols, circle - apart_cols)
    apart_rows = source_row[:, None] - target_row[None, :]
    square = (apart_cols * apart_cols + apart_rows * apart_rows).astype(jnp.float32)
    return jnp.exp(square * (-2.0 / (LON_DEV * LON_DEV)))

def gain_parts(sample_now, observed, noise):
    centre = lax.optimization_barrier(jnp.mean(sample_now, axis=0))
    spread = sample_now - centre
    covariance = jnp.dot(spread.T, spread, precision=highest) / (MEM - 1) + jnp.diag(noise)
    factor = jnp.linalg.cholesky(covariance)
    innovation = (observed - centre)[:, None]
    halfway = lax.linalg.triangular_solve(factor, innovation, left_side=True, lower=True)
    kalman_gain = lax.linalg.triangular_solve(factor, halfway, left_side=True, lower=True, transpose_a=True)[:, 0]
    rooted = factor + jnp.diag(jnp.sqrt(noise))
    identity = jnp.eye(OBS, dtype=noise.dtype)
    within = lax.linalg.triangular_solve(rooted, identity, left_side=True, lower=True)
    reduced = lax.linalg.triangular_solve(factor, within, left_side=True, lower=True, transpose_a=True)
    return (spread, kalman_gain, reduced)

def update_block(block, spread, kalman_gain, reduced, chosen, usable, obs_ids, local_ids, circle):
    levels = block.shape[1]
    rows_used = chosen.shape[0]
    weight = taper_weight(obs_ids[chosen], local_ids, circle) * usable[:, None]
    centre = lax.optimization_barrier(jnp.mean(block, axis=0))
    flattened = (block - centre).reshape(MEM, -1)
    crossed = jnp.dot(spread[:, chosen].T, flattened, precision=highest) / (MEM - 1)
    tapered = (crossed.reshape(rows_used, levels, -1) * weight[:, None, :]).reshape(rows_used, -1)
    shifted = jnp.dot(kalman_gain[chosen], tapered, precision=highest)
    mixing = jnp.dot(spread, reduced[chosen].T, precision=highest)
    flattened = flattened - jnp.dot(mixing, tapered, precision=highest)
    return ((centre.reshape(-1) + shifted)[None, :] + flattened).reshape(block.shape)

def reference(ensemble, obs_cell, obs_value, obs_noise, obs_weight, tile_lists, batch_order):
    circle = LON_DEV * N_LON
    tiles = ensemble.reshape(MEM, LEVELS, N_LON, CELL_DEV).transpose(2, 0, 1, 3)
    tile_ids = jnp.arange(N_LON, dtype=jnp.int32)

    def serial(tiles, position):
        current = batch_order[position]
        cell_ids = obs_cell[current]
        owners = cell_ids // CELL_DEV
        within = cell_ids % CELL_DEV
        picked = tiles[owners, :, :, within]
        probe = lax.optimization_barrier(jnp.sum(picked * obs_weight[current].T[:, None, :], axis=2)).T
        spread, kalman_gain, reduced = gain_parts(probe, obs_value[current], obs_noise[current])
        lists = tile_lists[current].reshape(N_LON, ROUTE_CAP)
        filled = (lists < OBS).astype(jnp.float32)
        safe = jnp.minimum(lists, OBS - 1).astype(jnp.int32)

        def single(items):
            block, chosen, usable, tile_index = items
            local_ids = tile_index * CELL_DEV + jnp.arange(CELL_DEV, dtype=jnp.int32)
            return update_block(block, spread, kalman_gain, reduced, chosen, usable, cell_ids, local_ids, circle)
        tiles = lax.map(single, (tiles, safe, filled, tile_ids))
        return (tiles, None)
    tiles, unused = lax.scan(serial, tiles, jnp.arange(BATCHES, dtype=jnp.int32))
    return tiles.transpose(1, 2, 0, 3).reshape(MEM, LEVELS, CELLS)
```

```python
import jax
import jax.numpy as jnp
from jax import lax
from jax.experimental import pallas as pl
from jax.experimental.pallas import tpu as pltpu
from jax.sharding import Mesh
from jax.sharding import PartitionSpec as P

MEM = 80
OBS = 128
ROUTE_CAP = 24
OWN_MAX = 8
LON_DEV = 16
CELL_DEV = 1024
BATCHES = 12
LEV_DEV = 8
ROWS = 32
LON = ("lon_0", "lon_1", "lon_2")
f32 = jnp.float32
bf16 = jnp.bfloat16


def sent_to_all(array, axis):
    copies = jnp.broadcast_to(array, (lax.axis_size(axis), *array.shape))
    return lax.all_to_all(copies, axis, split_axis=0, concat_axis=0, tiled=True)


def iota(shape, dim):
    return lax.broadcasted_iota(jnp.int32, shape, dim)


def split(x):
    high = x.astype(bf16)
    return high, (x - high.astype(f32)).astype(bf16)


def dot(a, b):
    return jnp.dot(a, b, preferred_element_type=f32)


def dot_lanes(a, b):
    return lax.dot_general(a, b, (((1,), (1,)), ((), ())), preferred_element_type=f32)


def lane_of(x, lane):
    return jnp.broadcast_to(x[:, lane : lane + 1], x.shape)


def sub_of(x, row):
    return jnp.broadcast_to(x[row : row + 1, :], x.shape)


def probe_kernel(tile_ref, ens_ref, table_ref, weight_ref, out_ref, turn_ref):
    tile = tile_ref[0]
    cells = table_ref[0:16, :].astype(jnp.int32)
    own = (cells >> 10) == tile
    lane = iota((OBS, OBS), 1)
    sub = iota((OBS, OBS), 0)
    before = (sub < lane).astype(f32).astype(bf16)
    rank = dot(own.astype(f32).astype(bf16), before)
    slot = jnp.where(own, iota((16, OBS), 0).astype(f32) * OWN_MAX + rank, -1.0)
    turn_ref[...] = jnp.zeros((OBS, OBS), f32)
    turn_ref[0:16, :] = slot
    slot_turned = turn_ref[...].T
    within = cells & (CELL_DEV - 1)
    row = (within >> 4).astype(f32)
    col = (within & 15).astype(f32)
    lane_f = lane.astype(f32)
    sub8 = iota((8, OBS), 0)
    picked = jnp.zeros((32, OBS), f32)
    for b in range(BATCHES):
        chosen = (lane_of(slot_turned, b) == lane_f).astype(f32).astype(bf16)
        weight = weight_ref[b]
        w_high = weight.astype(bf16).astype(f32)
        w_rest = weight - w_high
        w_mid = w_rest.astype(bf16).astype(f32)
        place = jnp.where(
            sub8 == 0,
            jnp.broadcast_to(row[b : b + 1, :], (8, OBS)),
            jnp.where(sub8 == 1, jnp.broadcast_to(col[b : b + 1, :], (8, OBS)), 0.0),
        )
        left = jnp.concatenate([place, w_high, w_mid, w_rest - w_mid], axis=0).astype(bf16)
        picked = picked + dot(left, chosen)
    cell = picked[0:1, :] * LON_DEV + picked[1:2, :]
    weight = picked[8:16, :] + picked[16:24, :] + picked[24:32, :]
    column = iota((CELL_DEV, OBS), 0).astype(f32)
    one_hot = (column == cell).astype(f32).astype(bf16)
    high, low = split(ens_ref[...])
    taken = dot(high, one_hot) + dot(low, one_hot)
    summed = jnp.sum(taken.reshape(MEM, LEV_DEV, OBS) * weight[None], axis=1)
    turn_ref[...] = jnp.zeros((OBS, OBS), f32)
    turn_ref[0:MEM, :] = summed
    out_ref[...] = turn_ref[...].T[0 : BATCHES * OWN_MAX, :]


def sweep(covariance, right, root):
    blocks = OBS // 8
    left_rows = [covariance[8 * i : 8 * i + 8, :] for i in range(blocks)]
    right_rows = [right[8 * i : 8 * i + 8, :] for i in range(blocks)]
    root_rows = [root[8 * i : 8 * i + 8, :] for i in range(blocks)]
    sub = iota((8, OBS), 0)
    for p in range(blocks):
        a, b, d = left_rows[p], right_rows[p], root_rows[p]
        columns = [lane_of(a, 8 * p + r) for r in range(8)]
        for j in range(8):
            pivot = sub_of(columns[j], j)
            inverse = 1.0 / pivot
            scale = 1.0 / (pivot + sub_of(d, j) * jnp.sqrt(pivot))
            at_j = sub == j
            row_a = sub_of(a, j) * inverse
            row_b = sub_of(b, j) * scale
            a = jnp.where(at_j, row_a, a - columns[j] * row_a)
            b = jnp.where(at_j, row_b, b - columns[j] * row_b)
            for r in range(j + 1, 8):
                row_c = sub_of(columns[r], j) * inverse
                columns[r] = jnp.where(at_j, row_c, columns[r] - columns[j] * row_c)
        left_rows[p], right_rows[p] = a, b
        rows_a = [sub_of(a, r) for r in range(8)]
        rows_b = [sub_of(b, r) for r in range(8)]
        for step in range(1, blocks):
            i = (p + step) % blocks
            old = left_rows[i]
            new_a, new_b = old, right_rows[i]
            for r in range(8):
                factor = lane_of(old, 8 * p + r)
                new_a = new_a - factor * rows_a[r]
                new_b = new_b - factor * rows_b[r]
            left_rows[i], right_rows[i] = new_a, new_b
    return jnp.concatenate(right_rows, axis=0)


def taper(rows_a, cols_a, rows_b, cols_b, circle):
    apart = jnp.abs(cols_a - cols_b)
    apart = jnp.minimum(apart, circle - apart)
    down = rows_a - rows_b
    return jnp.exp((apart * apart + down * down) * (-2.0 / (LON_DEV * LON_DEV)))


def serial_kernel(
    tiles,
    order_ref,
    tile_ref,
    probes_ref,
    table_ref,
    lists_ref,
    ens_ref,
    out_ref,
    raw_ref,
    state_ref,
    turn_ref,
    turn2_ref,
    rows_ref,
    paug_ref,
    row_ref,
    col_ref,
    tile_col_ref,
    value_ref,
    root_ref,
    noise_ref,
    listed_ref,
    weight_ref,
    sem,
):
    circle = float(LON_DEV * tiles)
    pieces = CELL_DEV // OBS

    def columns_of(ref, c):
        return ref.at[:, OBS * c : OBS * c + OBS]

    fetches = [pltpu.make_async_copy(columns_of(ens_ref, c), raw_ref.at[c], sem.at[c]) for c in range(pieces)]
    for fetch in fetches:
        fetch.start()
    square = (OBS, OBS)
    lane = iota(square, 1)
    sub = iota(square, 0)
    lane_f = lane.astype(f32)
    is_member = lane < MEM
    turn_ref[...] = jnp.zeros(square, f32)
    turn2_ref[...] = jnp.full(square, float(OBS), f32)
    for k in range(BATCHES):
        b = order_ref[k]
        for part in range(3):
            turn_ref[16 * part + k : 16 * part + k + 1, :] = table_ref[pl.ds(BATCHES * part + b, 1), :]
        turn2_ref[k : k + 1, 0:ROUTE_CAP] = lists_ref[pl.ds(b, 1), :]
    turned = turn_ref[...].T
    listed = turn2_ref[...].T
    cells = turn_ref[0:16, :].astype(jnp.int32)
    rows_ref[0] = ((cells & (CELL_DEV - 1)) >> 4).astype(f32)
    rows_ref[1] = ((cells >> 10) * LON_DEV + (cells & 15)).astype(f32)
    rows_ref[2] = (cells >> 10).astype(f32)
    ones = jnp.ones(square, f32).astype(bf16)
    for k in range(BATCHES):
        b = order_ref[k]
        cell = lane_of(turned, k).astype(jnp.int32)
        tile_col = (cell >> 10).astype(f32)
        row_ref[k] = ((cell & (CELL_DEV - 1)) >> 4).astype(f32)
        col_ref[k] = ((cell >> 10) * LON_DEV + (cell & 15)).astype(f32)
        tile_col_ref[k] = tile_col
        same = (tile_col == rows_ref[2, k : k + 1, :]) & (lane < sub)
        rank = dot(same.astype(f32).astype(bf16), ones)
        slot = tile_col * OWN_MAX + rank
        wide = tiles * OWN_MAX
        high, low = split(probes_ref[:, b].reshape(wide, OBS))
        gathered = jnp.zeros(square, f32)
        for c in range(wide // OBS):
            chosen = (slot == lane_f + float(OBS * c)).astype(f32).astype(bf16)
            part = slice(OBS * c, OBS * c + OBS)
            gathered = gathered + dot(chosen, high[part]) + dot(chosen, low[part])
        mean = jnp.sum(gathered, axis=1, keepdims=True) * (1.0 / MEM)
        mean = jnp.broadcast_to(mean, square)
        paug_ref[k] = jnp.where(is_member, gathered - mean, jnp.where(lane == MEM, mean, 0.0))
        value_ref[k] = lane_of(turned, 16 + k)
        noise = lane_of(turned, 32 + k)
        noise_ref[k] = jnp.where(lane == sub, noise, 0.0)
        root_ref[k] = jnp.where(is_member, jnp.sqrt(noise), 0.0)
        list_col = jnp.broadcast_to(listed[0:ROWS, k : k + 1], (ROWS, OBS))
        listed_ref[k] = (list_col == lane_f[0:ROWS]).astype(f32)
    for fetch in fetches:
        fetch.wait()
    for c in range(pieces):
        for level in range(LEV_DEV):
            state_ref[level, :, OBS * c : OBS * c + OBS] = raw_ref[c, pl.ds(level, MEM, stride=LEV_DEV), :]
    first_col = (tile_ref[0] * LON_DEV).astype(f32)
    here = iota((ROWS, CELL_DEV), 1)
    here_row = (here >> 4).astype(f32)
    here_col = (here & 15).astype(f32) + first_col

    def turn(k, carry):
        now = paug_ref[k]
        spread = jnp.where(is_member, now, 0.0)
        high, low = split(spread)
        covariance = dot_lanes(high, high) + dot_lanes(low, high) + dot_lanes(high, low)
        covariance = covariance * (1.0 / (MEM - 1)) + noise_ref[k]
        right = jnp.where(is_member, now, jnp.where(lane == MEM, value_ref[k] - now, 0.0))
        solved = sweep(covariance, right, root_ref[k])
        push = jnp.where(is_member, -solved, solved)
        push_high, push_low = split(push)

        source_row = rows_ref[0, pl.ds(k, 1), :]
        source_col = rows_ref[1, pl.ds(k, 1), :]
        source_tile = rows_ref[2, pl.ds(k, 1), :]

        def renew(other, carry):
            upcoming = paug_ref[other]
            up_high, up_low = split(jnp.where(is_member, upcoming, 0.0))
            crossed = dot_lanes(up_high, high) + dot_lanes(up_low, high) + dot_lanes(up_high, low)
            apart = jnp.abs(tile_col_ref[other] - source_tile)
            near = (apart <= 1.0) | (apart >= float(tiles - 1))
            weight = taper(row_ref[other], col_ref[other], source_row, source_col, circle)
            tapered = crossed * jnp.where(near, weight * (1.0 / (MEM - 1)), 0.0)
            t_high, t_low = split(tapered)
            change = dot(t_high, push_high) + dot(t_low, push_high) + dot(t_high, push_low)
            paug_ref[other] = upcoming + change
            return carry

        lax.fori_loop(k + 1, BATCHES, renew, 0)

        chosen_f = listed_ref[k]
        chosen = chosen_f.astype(bf16)
        s_high = dot(chosen, high)
        s_low = dot(chosen, low)
        lane_s = lane[0:ROWS]
        moved = pltpu.roll(s_high, MEM, 1)
        first = jnp.where(lane_s < MEM, s_high, moved)
        second = jnp.where(lane_s < 2 * MEM - OBS, moved, pltpu.roll(s_low, 2 * MEM - OBS, 1))
        left = jnp.concatenate([first, second], axis=1).astype(bf16)
        gain = dot(chosen, push_high) + dot(chosen, push_low)
        gain = jnp.where(lane_s < MEM, gain + lane_of(gain, MEM), 0.0)
        gain_high = gain.astype(bf16).astype(f32)
        stacked = jnp.concatenate([gain_high, gain_high, gain - gain_high, jnp.zeros_like(gain)], axis=0)
        mixing = stacked.T[0:MEM, :].astype(bf16)
        row_of = jnp.sum(chosen_f * source_row, axis=1, keepdims=True)
        col_of = jnp.sum(chosen_f * source_col, axis=1, keepdims=True)
        weight_ref[...] = taper(row_of, col_of, here_row, here_col, circle) * (1.0 / (MEM - 1))

        def renew_level(level, carry):
            block = state_ref[level]
            x_high, x_low = split(block)
            filler = jnp.zeros((16, CELL_DEV), bf16)
            crossed = dot(left, jnp.concatenate([x_high, x_low, x_high, filler], axis=0))
            tapered = crossed * weight_ref[...]
            t_high, t_low = split(tapered)
            filler = jnp.zeros((ROWS, CELL_DEV), bf16)
            change = dot(mixing, jnp.concatenate([t_high, t_low, t_high, filler], axis=0))
            state_ref[level] = block + change
            return carry

        lax.fori_loop(0, LEV_DEV, renew_level, 0)
        return carry

    lax.fori_loop(0, BATCHES, turn, 0)
    stores = [pltpu.make_async_copy(raw_ref.at[c], columns_of(out_ref, c), sem.at[c]) for c in range(pieces)]
    for c in range(pieces):
        for level in range(LEV_DEV):
            raw_ref[c, pl.ds(level, MEM, stride=LEV_DEV), :] = state_ref[level, :, OBS * c : OBS * c + OBS]
        stores[c].start()
    for store in stores:
        store.wait()


def whole(space):
    return pl.BlockSpec(memory_space=space)


def body(ensemble, obs_cell, obs_value, obs_noise, obs_weight, tile_lists, batch_order):
    tiles = lax.axis_size(LON)
    tile = jnp.reshape(lax.axis_index(LON), (1,)).astype(jnp.int32)
    mine = jnp.concatenate([obs_cell.astype(f32), obs_value, obs_noise], axis=0)
    table = sent_to_all(mine, LON)
    table = jnp.moveaxis(table, 0, 1).reshape(3 * BATCHES, OBS)
    flat = ensemble.reshape(MEM * LEV_DEV, CELL_DEV)
    slots = BATCHES * OWN_MAX
    portion = pl.pallas_call(
        probe_kernel,
        name="probe_kernel",
        out_shape=jax.ShapeDtypeStruct((slots, OBS), f32),
        in_specs=[whole(pltpu.SMEM), whole(pltpu.VMEM), whole(pltpu.VMEM), whole(pltpu.VMEM)],
        out_specs=whole(pltpu.VMEM),
        scratch_shapes=[pltpu.VMEM((OBS, OBS), f32)],
        compiler_params=pltpu.CompilerParams(vmem_limit_bytes=32 << 20),
    )(tile, flat, table, obs_weight)
    portion = lax.psum(portion, "lev")
    probes = sent_to_all(portion, LON).reshape(tiles, BATCHES, OWN_MAX, OBS)
    square = (BATCHES, OBS, OBS)

    def run(*refs):
        serial_kernel(tiles, *refs)

    result = pl.pallas_call(
        run,
        name="serial_kernel",
        out_shape=jax.ShapeDtypeStruct(flat.shape, f32),
        in_specs=[
            whole(pltpu.SMEM),
            whole(pltpu.SMEM),
            whole(pltpu.VMEM),
            whole(pltpu.VMEM),
            whole(pltpu.VMEM),
            whole(pl.ANY),
        ],
        out_specs=whole(pl.ANY),
        scratch_shapes=[
            pltpu.VMEM((CELL_DEV // OBS, MEM * LEV_DEV, OBS), f32),
            pltpu.VMEM((LEV_DEV, MEM, CELL_DEV), f32),
            pltpu.VMEM((OBS, OBS), f32),
            pltpu.VMEM((OBS, OBS), f32),
            pltpu.VMEM((3, 16, OBS), f32),
            pltpu.VMEM(square, f32),
            pltpu.VMEM(square, f32),
            pltpu.VMEM(square, f32),
            pltpu.VMEM(square, f32),
            pltpu.VMEM(square, f32),
            pltpu.VMEM(square, f32),
            pltpu.VMEM(square, f32),
            pltpu.VMEM((BATCHES, ROWS, OBS), f32),
            pltpu.VMEM((ROWS, CELL_DEV), f32),
            pltpu.SemaphoreType.DMA((CELL_DEV // OBS,)),
        ],
        compiler_params=pltpu.CompilerParams(vmem_limit_bytes=48 << 20),
    )(batch_order, tile, probes, table, tile_lists.astype(f32), flat)
    return result.reshape(MEM, LEV_DEV, CELL_DEV)


def solution(mesh):
    finer = Mesh(
        mesh.devices.reshape(4, 4, 4, mesh.shape["lev"]), ("lon_0", "lon_1", "lon_2", "lev")
    )
    in_specs = (
        P(None, "lev", LON),
        P(None, LON),
        P(None, LON),
        P(None, LON),
        P(None, "lev", None),
        P(None, LON),
        P(),
    )
    out_specs = P(None, "lev", LON)
    return jax.shard_map(body, mesh=finer, in_specs=in_specs, out_specs=out_specs, check_vma=False)
```

```python
import jax
import jax.numpy as jnp
from jax import lax
from jax.experimental import pallas as pl
from jax.experimental.pallas import tpu as pltpu
from jax.sharding import Mesh
from jax.sharding import PartitionSpec as P

MEM = 80
OBS = 128
ROUTE_CAP = 24
OWN_MAX = 8
LON_DEV = 16
CELL_DEV = 1024
BATCHES = 12
LEV_DEV = 8
ROWS = 32
HALF = 6
PACK = 32
SEGMENT = 12
LON = ("lon_0", "lon_1", "lon_2")
f32 = jnp.float32
bf16 = jnp.bfloat16


def sent_to_all(array, axis):
    copies = jnp.broadcast_to(array, (lax.axis_size(axis), *array.shape))
    return lax.all_to_all(copies, axis, split_axis=0, concat_axis=0, tiled=True)


def iota(shape, dim):
    return lax.broadcasted_iota(jnp.int32, shape, dim)


def split(x):
    high = x.astype(bf16)
    return high, (x - high.astype(f32)).astype(bf16)


def dot(a, b):
    return jnp.dot(a, b, preferred_element_type=f32)


def dot_lanes(a, b):
    return lax.dot_general(a, b, (((1,), (1,)), ((), ())), preferred_element_type=f32)


def lane_of(x, lane):
    return jnp.broadcast_to(x[:, lane : lane + 1], x.shape)


def sub_of(x, row):
    return jnp.broadcast_to(x[row : row + 1, :], x.shape)


def probe_kernel(place_ref, ens_ref, table_ref, weight_ref, keep_ref, send_ref, turn_ref, block_ref, sem):
    tile, level_half = place_ref[0], place_ref[1]
    fetch = pltpu.make_async_copy(ens_ref, block_ref, sem)
    fetch.start()
    cells = table_ref[0:16, :].astype(jnp.int32)
    own = (cells >> 10) == tile
    lane = iota((OBS, OBS), 1)
    sub = iota((OBS, OBS), 0)
    before = (sub < lane).astype(f32).astype(bf16)
    rank = dot(own.astype(f32).astype(bf16), before)
    slot = jnp.where(own, iota((16, OBS), 0).astype(f32) * OWN_MAX + rank, -1.0)
    turn_ref[...] = jnp.zeros((OBS, OBS), f32)
    turn_ref[0:16, :] = slot
    slot_turned = turn_ref[...].T
    within = cells & (CELL_DEV - 1)
    row = (within >> 4).astype(f32)
    col = (within & 15).astype(f32)
    lane_f = lane.astype(f32)
    sub8 = iota((8, OBS), 0)
    picked = jnp.zeros((32, OBS), f32)
    for b in range(BATCHES):
        chosen = (lane_of(slot_turned, b) == lane_f).astype(f32).astype(bf16)
        weight = weight_ref[b]
        w_high = weight.astype(bf16).astype(f32)
        w_rest = weight - w_high
        w_mid = w_rest.astype(bf16).astype(f32)
        place = jnp.where(
            sub8 == 0,
            jnp.broadcast_to(row[b : b + 1, :], (8, OBS)),
            jnp.where(sub8 == 1, jnp.broadcast_to(col[b : b + 1, :], (8, OBS)), 0.0),
        )
        left = jnp.concatenate([place, w_high, w_mid, w_rest - w_mid], axis=0).astype(bf16)
        picked = picked + dot(left, chosen)
    cell = picked[0:1, :] * LON_DEV + picked[1:2, :]
    weight = picked[8:16, :] + picked[16:24, :] + picked[24:32, :]
    column = iota((CELL_DEV, OBS), 0).astype(f32)
    one_hot = (column == cell).astype(f32).astype(bf16)
    fetch.wait()
    high, low = split(block_ref[...])
    taken = dot(high, one_hot) + dot(low, one_hot)
    summed = jnp.sum(taken.reshape(MEM, LEV_DEV, OBS) * weight[None], axis=1)
    turn_ref[...] = jnp.zeros((OBS, OBS), f32)
    turn_ref[0:MEM, :] = summed
    turn_ref[...] = turn_ref[...].T
    lane6 = iota((HALF, OBS), 1)
    for half, out_ref in ((level_half, keep_ref), (1 - level_half, send_ref)):
        first = half * (HALF * OWN_MAX)
        slots = [turn_ref[pl.ds(first + s, HALF, stride=OWN_MAX), :] for s in range(OWN_MAX)]
        out_ref[...] = jnp.zeros((PACK, OBS), f32)
        tail = jnp.zeros((HALF, OBS), f32)
        for r in range(4):
            both = jnp.where(lane6 < 64, slots[r], pltpu.roll(slots[r + 4], 64, 1))
            out_ref[HALF * r : HALF * r + HALF, :] = both
        for s in range(OWN_MAX):
            tail = jnp.where((lane6 >> 4) == s, pltpu.roll(slots[s], (16 * s + 64) % OBS, 1), tail)
        out_ref[HALF * 4 : HALF * 5, :] = tail


def sweep(covariance, right, root, fill):
    blocks = OBS // 8
    left_rows = [covariance[8 * i : 8 * i + 8, :] for i in range(blocks)]
    right_rows = [right[8 * i : 8 * i + 8, :] for i in range(blocks)]
    root_rows = [root[8 * i : 8 * i + 8, :] for i in range(blocks)]
    sub = iota((8, OBS), 0)
    for p in range(blocks):
        a, b, d = left_rows[p], right_rows[p], root_rows[p]
        columns = [lane_of(a, 8 * p + r) for r in range(8)]
        scale = jnp.ones((8, OBS), f32)
        for j in range(8):
            at_j = sub == j
            pivot = sub_of(columns[j], j)
            inverse = 1.0 / pivot
            others = jnp.where(at_j, 0.0, columns[j])
            factor = others * inverse
            if j < 7:
                ahead = others * sub_of(columns[j + 1], j)
                columns[j + 1] = columns[j + 1] - ahead * inverse
            for r in range(j + 2, 8):
                columns[r] = columns[r] - factor * sub_of(columns[r], j)
            a = a - factor * sub_of(a, j)
            b = b * jnp.where(at_j, 1.0 / (1.0 + sub_of(d, j) * lax.rsqrt(pivot)), 1.0)
            b = b - factor * sub_of(b, j)
            scale = jnp.where(at_j, inverse, scale)
        a, b = a * scale, b * scale
        left_rows[p], right_rows[p] = a, b
        rows_a = [sub_of(a, r) for r in range(8)]
        rows_b = [sub_of(b, r) for r in range(8)]
        for step in range(1, blocks):
            i = (p + step) % blocks
            old = left_rows[i]
            new_a, new_b = old, right_rows[i]
            for r in range(8):
                factor = lane_of(old, 8 * p + r)
                if p < blocks - 1:
                    new_a = new_a - factor * rows_a[r]
                new_b = new_b - factor * rows_b[r]
            left_rows[i], right_rows[i] = new_a, new_b
        fill(p)
    return jnp.concatenate(right_rows, axis=0)


def covariance_of(spread):
    high = spread.astype(bf16)
    rest = spread - high.astype(f32)
    mid = rest.astype(bf16)
    low = (rest - mid.astype(f32)).astype(bf16)
    small = dot_lanes(high, low) + dot_lanes(low, high) + dot_lanes(mid, mid)
    return dot_lanes(high, high) + (dot_lanes(high, mid) + dot_lanes(mid, high) + small)


def taper(rows_a, cols_a, rows_b, cols_b, circle):
    apart = jnp.abs(cols_a - cols_b)
    apart = jnp.minimum(apart, circle - apart)
    down = rows_a - rows_b
    return jnp.exp((apart * apart + down * down) * (-2.0 / (LON_DEV * LON_DEV)))


def pair_index(k, other):
    return k * (2 * BATCHES - 1 - k) // 2 + other - k - 1


def index_kernel(
    tiles,
    order_ref,
    place_ref,
    after_ref,
    table_ref,
    lists_ref,
    ens_ref,
    state_ref,
    pair_ref,
    local_ref,
    listed_ref,
    rank_ref,
    tile_col_ref,
    value_ref,
    root_ref,
    noise_ref,
    token_ref,
    raw_ref,
    turn_ref,
    turn2_ref,
    rows_ref,
    row_ref,
    col_ref,
    sem,
):
    circle = float(LON_DEV * tiles)
    pieces = CELL_DEV // OBS
    fetches = [
        pltpu.make_async_copy(ens_ref.at[:, OBS * c : OBS * c + OBS], raw_ref.at[c], sem.at[c])
        for c in range(pieces)
    ]
    for fetch in fetches:
        fetch.start()
    token_ref[...] = jnp.zeros((8, OBS), f32)
    listed_ref[BATCHES] = jnp.zeros((ROWS, OBS), f32)
    square = (OBS, OBS)
    lane = iota(square, 1)
    sub = iota(square, 0)
    lane_f = lane.astype(f32)
    turn_ref[...] = jnp.zeros(square, f32)
    turn2_ref[...] = jnp.full(square, float(OBS), f32)
    for k in range(BATCHES):
        b = order_ref[k]
        for part in range(3):
            turn_ref[16 * part + k : 16 * part + k + 1, :] = table_ref[pl.ds(BATCHES * part + b, 1), :]
        turn2_ref[k : k + 1, 0:ROUTE_CAP] = lists_ref[pl.ds(b, 1), :].astype(f32)
    turned = turn_ref[...].T
    listed = turn2_ref[...].T
    cells = turn_ref[0:16, :].astype(jnp.int32)
    rows_ref[0] = ((cells & (CELL_DEV - 1)) >> 4).astype(f32)
    rows_ref[1] = ((cells >> 10) * LON_DEV + (cells & 15)).astype(f32)
    rows_ref[2] = (cells >> 10).astype(f32)
    ones = jnp.ones(square, f32).astype(bf16)
    first_col = (place_ref[0] * LON_DEV).astype(f32)
    here = iota((ROWS, CELL_DEV), 1)
    here_row = (here >> 4).astype(f32)
    here_col = (here & 15).astype(f32) + first_col
    for k in range(BATCHES):
        cell = lane_of(turned, k).astype(jnp.int32)
        tile_col = (cell >> 10).astype(f32)
        row_ref[k] = ((cell & (CELL_DEV - 1)) >> 4).astype(f32)
        col_ref[k] = ((cell >> 10) * LON_DEV + (cell & 15)).astype(f32)
        tile_col_ref[k] = tile_col
        same = (tile_col == rows_ref[2, k : k + 1, :]) & (lane < sub)
        rank_ref[k] = dot(same.astype(f32).astype(bf16), ones)
        value_ref[k] = lane_of(turned, 16 + k)
        noise = lane_of(turned, 32 + k)
        noise_ref[k] = jnp.where(lane == sub, noise, 0.0)
        root_ref[k] = jnp.where(lane < MEM, jnp.sqrt(noise), 0.0)
        list_col = jnp.broadcast_to(listed[0:ROWS, k : k + 1], (ROWS, OBS))
        chosen = (list_col == lane_f[0:ROWS]).astype(f32)
        listed_ref[k] = chosen
        row_of = jnp.sum(chosen * rows_ref[0, k : k + 1, :], axis=1, keepdims=True)
        col_of = jnp.sum(chosen * rows_ref[1, k : k + 1, :], axis=1, keepdims=True)
        local_ref[k] = taper(row_of, col_of, here_row, here_col, circle) * (1.0 / (MEM - 1))

    def pairs(k, carry):
        source_row = rows_ref[0, pl.ds(k, 1), :]
        source_col = rows_ref[1, pl.ds(k, 1), :]
        source_tile = rows_ref[2, pl.ds(k, 1), :]

        def pair(other, carry):
            apart = jnp.abs(tile_col_ref[other] - source_tile)
            near = (apart <= 1.0) | (apart >= float(tiles - 1))
            weight = taper(row_ref[other], col_ref[other], source_row, source_col, circle)
            pair_ref[pair_index(k, other)] = jnp.where(near, weight * (1.0 / (MEM - 1)), 0.0)
            return carry

        return lax.fori_loop(k + 1, BATCHES, pair, carry)

    lax.fori_loop(0, BATCHES, pairs, 0)
    for fetch in fetches:
        fetch.wait()
    for c in range(pieces):
        for level in range(LEV_DEV):
            state_ref[level, :, OBS * c : OBS * c + OBS] = raw_ref[c, pl.ds(level, MEM, stride=LEV_DEV), :]


def serial_kernel(
    tiles,
    order_ref,
    place_ref,
    mine_ref,
    other_ref,
    token_ref,
    state_sent,
    pair_sent,
    local_sent,
    listed_sent,
    rank_sent,
    tile_col_sent,
    value_sent,
    root_sent,
    noise_sent,
    out_ref,
    state_ref,
    pair_ref,
    local_ref,
    listed_ref,
    rank_ref,
    tile_col_ref,
    value_ref,
    root_ref,
    noise_ref,
    raw_ref,
    paug_ref,
    past_ref,
    sem,
    sent_sem,
):
    moves = (
        (tile_col_sent, tile_col_ref),
        (rank_sent, rank_ref),
        (noise_sent, noise_ref),
        (value_sent, value_ref),
        (root_sent, root_ref),
        (listed_sent, listed_ref),
        (local_sent, local_ref),
        (pair_sent, pair_ref),
        (state_sent, state_ref),
    )
    fetches = [pltpu.make_async_copy(a, b, sent_sem.at[n]) for n, (a, b) in enumerate(moves)]
    for fetch in fetches:
        fetch.start()
    for fetch in fetches[:2]:
        fetch.wait()
    pieces = CELL_DEV // OBS
    square = (OBS, OBS)
    lane = iota(square, 1)
    lane_f = lane.astype(f32)
    is_member = lane < MEM
    group = lane >> 4
    fold = (lane == 64 + (iota(square, 0) & 15)).astype(f32).astype(bf16)
    lane_t = lane_f[:, 0:tiles]
    for k in range(BATCHES):
        b = order_ref[k]
        half = b // HALF
        here = b - half * HALF
        from_mine = half == place_ref[1]
        rank = rank_ref[k].astype(jnp.int32)
        chosen = (tile_col_ref[k, :, 0:tiles] == lane_t).astype(f32).astype(bf16)
        sent = []
        for r in range(5):
            rows = pl.ds(HALF * r + here, tiles, stride=PACK)
            sent.extend(split(jnp.where(from_mine, mine_ref[rows, :], other_ref[rows, :])))
        taken = dot(chosen, jnp.concatenate(sent, axis=1))
        parts = [taken[:, OBS * c : OBS * c + OBS] for c in range(10)]
        body = parts[0] + parts[1]
        for r in range(1, 4):
            body = jnp.where((rank & 3) == r, parts[2 * r] + parts[2 * r + 1], body)
        body = jnp.where(rank >= 4, pltpu.roll(body, 64, 1), body)
        at_rank = group == rank
        tail = dot(jnp.where(at_rank, parts[8], 0.0).astype(bf16), fold)
        tail = tail + dot(jnp.where(at_rank, parts[9], 0.0).astype(bf16), fold)
        gathered = jnp.where(lane < 64, body, tail)
        gathered = jnp.where(is_member, gathered, 0.0)
        mean = jnp.sum(gathered, axis=1, keepdims=True) * (1.0 / MEM)
        mean = jnp.broadcast_to(mean, square)
        paug_ref[k] = jnp.where(is_member, gathered - mean, jnp.where(lane == MEM, mean, 0.0))
    for fetch in fetches[2:]:
        fetch.wait()

    is_member_s = is_member[0:ROWS]
    lane_s = lane[0:ROWS]
    last_pair = pair_ref.shape[0] - 1
    for extra in range(BATCHES, 2 * BATCHES):
        paug_ref[extra] = jnp.zeros(square, f32)
    for part in range(4):
        past_ref[part] = jnp.zeros(square, bf16)

    def operators():
        high, low, push_high, push_low = (past_ref[part] for part in range(4))
        chosen = listed_ref[BATCHES].astype(bf16)
        s_high = dot(chosen, high)
        s_low = dot(chosen, low)
        moved = pltpu.roll(s_high, MEM, 1)
        first = jnp.where(is_member_s, s_high, moved)
        second = jnp.where(lane_s < 2 * MEM - OBS, moved, pltpu.roll(s_low, 2 * MEM - OBS, 1))
        left = jnp.concatenate([first, second], axis=1).astype(bf16)
        gain = dot(chosen, push_high) + dot(chosen, push_low)
        gain = jnp.where(is_member_s, gain + lane_of(gain, MEM), 0.0)
        gain_high = gain.astype(bf16).astype(f32)
        stacked = jnp.concatenate([gain_high, gain_high, gain - gain_high, jnp.zeros_like(gain)], axis=0)
        return left, stacked.T[0:MEM, :].astype(bf16)

    def renew_level(level, before, left, mixing):
        block = state_ref[level]
        x_high, x_low = split(block)
        filler = jnp.zeros((16, CELL_DEV), bf16)
        crossed = dot(left, jnp.concatenate([x_high, x_low, x_high, filler], axis=0))
        tapered = crossed * local_ref[before]
        t_high, t_low = split(tapered)
        filler = jnp.zeros((ROWS, CELL_DEV), bf16)
        change = dot(mixing, jnp.concatenate([t_high, t_low, t_high, filler], axis=0))
        state_ref[level] = block + change

    def tapered_by(upcoming, high, low, pair):
        up_high, up_low = split(jnp.where(is_member, upcoming, 0.0))
        crossed = dot_lanes(up_high, high) + dot_lanes(up_low, high) + dot_lanes(up_high, low)
        return split(crossed * pair_ref[jnp.clip(pair, 0, last_pair)])

    def pushed(parts, push_high, push_low):
        t_high, t_low = parts
        return dot(t_high, push_high) + dot(t_low, push_high) + dot(t_high, push_low)

    def turn(k, slots):
        before = jnp.maximum(k - 1, 0)
        now = paug_ref[k]
        spread = jnp.where(is_member, now, 0.0)
        high, low = split(spread)
        old_high, old_low, old_push_high, old_push_low = (past_ref[part] for part in range(4))
        left, mixing = operators()
        covariance = covariance_of(spread) * (1.0 / (MEM - 1)) + noise_ref[k]
        right = jnp.where(is_member, now, jnp.where(lane == MEM, value_ref[k] - now, 0.0))
        ready = []

        def fill(p):
            if p < slots:
                other = k + 1 + p
                upcoming = paug_ref[other]
                parts = tapered_by(upcoming, old_high, old_low, pair_index(k - 1, other))
                upcoming = upcoming + pushed(parts, old_push_high, old_push_low)
                paug_ref[other] = upcoming
                if p == 0:
                    ready.append(upcoming)
                    ready.append(tapered_by(upcoming, high, low, pair_index(k, other)))
            if p % 2 == 1:
                renew_level(p // 2, before, left, mixing)

        solved = sweep(covariance, right, root_ref[k], fill)
        push = jnp.where(is_member, -solved, solved)
        push_high, push_low = split(push)
        paug_ref[k + 1] = ready[0] + pushed(ready[1], push_high, push_low)
        for part, value in enumerate((high, low, push_high, push_low)):
            past_ref[part] = value
        listed_ref[BATCHES] = listed_ref[k]

    for start in range(0, BATCHES, SEGMENT):

        def step(k, carry):
            turn(k, BATCHES - 1 - start)
            return carry

        lax.fori_loop(start, start + SEGMENT, step, 0)
    left, mixing = operators()
    for level in range(LEV_DEV):
        renew_level(level, BATCHES - 1, left, mixing)
    stores = [
        pltpu.make_async_copy(raw_ref.at[c], out_ref.at[:, OBS * c : OBS * c + OBS], sem.at[c])
        for c in range(pieces)
    ]
    for c in range(pieces):
        for level in range(LEV_DEV):
            raw_ref[c, pl.ds(level, MEM, stride=LEV_DEV), :] = state_ref[level, :, OBS * c : OBS * c + OBS]
        stores[c].start()
    for store in stores:
        store.wait()


def whole(space):
    return pl.BlockSpec(memory_space=space)


def body(ensemble, obs_cell, obs_value, obs_noise, obs_weight, tile_lists, batch_order):
    tiles = lax.axis_size(LON)
    place = jnp.stack([lax.axis_index(LON), lax.axis_index("lev")]).astype(jnp.int32)
    mine = jnp.concatenate([obs_cell.astype(f32), obs_value, obs_noise], axis=0)
    table = sent_to_all(mine, LON)
    table = jnp.moveaxis(table, 0, 1).reshape(3 * BATCHES, OBS)
    flat = ensemble.reshape(MEM * LEV_DEV, CELL_DEV)
    packed = jax.ShapeDtypeStruct((PACK, OBS), f32)
    keep, send = pl.pallas_call(
        probe_kernel,
        name="probe_kernel",
        out_shape=(packed, packed),
        in_specs=[whole(pltpu.SMEM), whole(pl.ANY), whole(pltpu.VMEM), whole(pltpu.VMEM)],
        out_specs=(whole(pltpu.VMEM), whole(pltpu.VMEM)),
        scratch_shapes=[
            pltpu.VMEM((OBS, OBS), f32),
            pltpu.VMEM(flat.shape, f32),
            pltpu.SemaphoreType.DMA,
        ],
        compiler_params=pltpu.CompilerParams(vmem_limit_bytes=62 << 20),
    )(place, flat, table, obs_weight)
    swap = [(0, 1), (1, 0)]
    portion = keep + lax.ppermute(send, "lev", swap)
    mine = sent_to_all(portion, LON)
    square = (BATCHES, OBS, OBS)
    pair_count = BATCHES * (BATCHES - 1) // 2
    state_shape = (LEV_DEV, MEM, CELL_DEV)
    raw_shape = (CELL_DEV // OBS, MEM * LEV_DEV, OBS)

    def index_run(*refs):
        given, sent, token, held, rest = refs[:6], refs[6:15], refs[15], refs[16:25], refs[25:]
        index_kernel(tiles, *given, *held, token, *rest[:-1])
        copies = [pltpu.make_async_copy(a, b, rest[-1].at[n]) for n, (a, b) in enumerate(zip(held, sent))]
        for copy in copies:
            copy.start()
        for copy in copies:
            copy.wait()

    shapes = (
        state_shape,
        (pair_count, OBS, OBS),
        (BATCHES, ROWS, CELL_DEV),
        (BATCHES + 1, ROWS, OBS),
        square,
        square,
        square,
        square,
        square,
        (8, OBS),
    )
    known = pl.pallas_call(
        index_run,
        name="index_kernel",
        out_shape=tuple(jax.ShapeDtypeStruct(shape, f32) for shape in shapes),
        in_specs=[whole(pltpu.SMEM)] * 2 + [whole(pltpu.VMEM)] * 3 + [whole(pl.ANY)],
        out_specs=tuple(whole(pltpu.HBM) for shape in shapes[:-1]) + (whole(pltpu.VMEM),),
        scratch_shapes=[pltpu.VMEM(shape, f32) for shape in shapes[:-1]]
        + [
            pltpu.VMEM(raw_shape, f32),
            pltpu.VMEM((OBS, OBS), f32),
            pltpu.VMEM((OBS, OBS), f32),
            pltpu.VMEM((3, 16, OBS), f32),
            pltpu.VMEM(square, f32),
            pltpu.VMEM(square, f32),
            pltpu.SemaphoreType.DMA((CELL_DEV // OBS,)),
            pltpu.SemaphoreType.DMA((len(shapes) - 1,)),
        ],
        cost_estimate=pl.CostEstimate(flops=40 << 20, transcendentals=2 << 20, bytes_accessed=16 << 20),
        compiler_params=pltpu.CompilerParams(vmem_limit_bytes=62 << 20),
    )(batch_order, place, portion, table, tile_lists, flat)
    mine, token = lax.optimization_barrier((mine, known[-1]))
    known = (*known[:-1], token)
    other = lax.ppermute(mine, "lev", swap)
    mine = mine.reshape(tiles * PACK, OBS)
    other = other.reshape(tiles * PACK, OBS)

    def run(*refs):
        serial_kernel(tiles, *refs)

    result = pl.pallas_call(
        run,
        name="serial_kernel",
        out_shape=jax.ShapeDtypeStruct(flat.shape, f32),
        in_specs=[whole(pltpu.SMEM)] * 2
        + [whole(pltpu.VMEM)] * 3
        + [whole(pltpu.HBM)] * 9,
        out_specs=whole(pl.ANY),
        scratch_shapes=[pltpu.VMEM(shape, f32) for shape in shapes[:-1]]
        + [
            pltpu.VMEM(raw_shape, f32),
            pltpu.VMEM((2 * BATCHES, OBS, OBS), f32),
            pltpu.VMEM((4, OBS, OBS), bf16),
            pltpu.SemaphoreType.DMA((CELL_DEV // OBS,)),
            pltpu.SemaphoreType.DMA((len(shapes) - 1,)),
        ],
        compiler_params=pltpu.CompilerParams(vmem_limit_bytes=60 << 20),
    )(batch_order, place, mine, other, known[-1], *known[:-1])
    return result.reshape(MEM, LEV_DEV, CELL_DEV)


def solution(mesh):
    finer = Mesh(
        mesh.devices.reshape(4, 4, 4, mesh.shape["lev"]), ("lon_0", "lon_1", "lon_2", "lev")
    )
    in_specs = (
        P(None, "lev", LON),
        P(None, LON),
        P(None, LON),
        P(None, LON),
        P(None, "lev", None),
        P(None, LON),
        P(),
    )
    out_specs = P(None, "lev", LON)
    return jax.shard_map(body, mesh=finer, in_specs=in_specs, out_specs=out_specs, check_vma=False)
```

```python
import jax
import jax.numpy as jnp
from jax import lax
from jax.experimental import pallas as pl
from jax.experimental.pallas import tpu as pltpu
from jax.sharding import Mesh
from jax.sharding import PartitionSpec as P

MEM = 80
OBS = 128
ROUTE_CAP = 24
OWN_MAX = 8
LON_DEV = 16
CELL_DEV = 1024
BATCHES = 12
LEV_DEV = 8
ROWS = 32
HALF = 6
PACK = 32
SEGMENT = 4
LAG = 3
WIDE = 16
LEVEL_TURNS = (2, 4, 6, 8, 10, 11, 12, 13)
LON = ("lon_0", "lon_1", "lon_2")
f32 = jnp.float32
bf16 = jnp.bfloat16


def sent_to_all(array, axis):
    copies = jnp.broadcast_to(array, (lax.axis_size(axis), *array.shape))
    return lax.all_to_all(copies, axis, split_axis=0, concat_axis=0, tiled=True)


def iota(shape, dim):
    return lax.broadcasted_iota(jnp.int32, shape, dim)


def split(x):
    high = x.astype(bf16)
    return high, (x - high.astype(f32)).astype(bf16)


def dot(a, b):
    return jnp.dot(a, b, preferred_element_type=f32)


def dot_lanes(a, b):
    return lax.dot_general(a, b, (((1,), (1,)), ((), ())), preferred_element_type=f32)


def lane_of(x, lane):
    return jnp.broadcast_to(x[:, lane : lane + 1], x.shape)


def sub_of(x, row):
    return jnp.broadcast_to(x[row : row + 1, :], x.shape)


def probe_kernel(place_ref, ens_ref, table_ref, weight_ref, keep_ref, send_ref, turn_ref, block_ref, sem):
    tile, level_half = place_ref[0], place_ref[1]
    fetch = pltpu.make_async_copy(ens_ref, block_ref, sem)
    fetch.start()
    cells = table_ref[0:16, :].astype(jnp.int32)
    own = (cells >> 10) == tile
    lane = iota((OBS, OBS), 1)
    sub = iota((OBS, OBS), 0)
    before = (sub < lane).astype(f32).astype(bf16)
    rank = dot(own.astype(f32).astype(bf16), before)
    slot = jnp.where(own, iota((16, OBS), 0).astype(f32) * OWN_MAX + rank, -1.0)
    turn_ref[...] = jnp.zeros((OBS, OBS), f32)
    turn_ref[0:16, :] = slot
    slot_turned = turn_ref[...].T
    within = cells & (CELL_DEV - 1)
    row = (within >> 4).astype(f32)
    col = (within & 15).astype(f32)
    lane_f = lane.astype(f32)
    sub8 = iota((8, OBS), 0)
    picked = jnp.zeros((32, OBS), f32)
    for b in range(BATCHES):
        chosen = (lane_of(slot_turned, b) == lane_f).astype(f32).astype(bf16)
        weight = weight_ref[b]
        w_high = weight.astype(bf16).astype(f32)
        w_rest = weight - w_high
        w_mid = w_rest.astype(bf16).astype(f32)
        place = jnp.where(
            sub8 == 0,
            jnp.broadcast_to(row[b : b + 1, :], (8, OBS)),
            jnp.where(sub8 == 1, jnp.broadcast_to(col[b : b + 1, :], (8, OBS)), 0.0),
        )
        left = jnp.concatenate([place, w_high, w_mid, w_rest - w_mid], axis=0).astype(bf16)
        picked = picked + dot(left, chosen)
    cell = picked[0:1, :] * LON_DEV + picked[1:2, :]
    weight = picked[8:16, :] + picked[16:24, :] + picked[24:32, :]
    column = iota((CELL_DEV, OBS), 0).astype(f32)
    one_hot = (column == cell).astype(f32).astype(bf16)
    fetch.wait()
    high, low = split(block_ref[...])
    taken = dot(high, one_hot) + dot(low, one_hot)
    summed = jnp.sum(taken.reshape(MEM, LEV_DEV, OBS) * weight[None], axis=1)
    turn_ref[...] = jnp.zeros((OBS, OBS), f32)
    turn_ref[0:MEM, :] = summed
    turn_ref[...] = turn_ref[...].T
    lane6 = iota((HALF, OBS), 1)
    for half, out_ref in ((level_half, keep_ref), (1 - level_half, send_ref)):
        first = half * (HALF * OWN_MAX)
        slots = [turn_ref[pl.ds(first + s, HALF, stride=OWN_MAX), :] for s in range(OWN_MAX)]
        out_ref[...] = jnp.zeros((PACK, OBS), f32)
        tail = jnp.zeros((HALF, OBS), f32)
        for r in range(4):
            both = jnp.where(lane6 < 64, slots[r], pltpu.roll(slots[r + 4], 64, 1))
            out_ref[HALF * r : HALF * r + HALF, :] = both
        for s in range(OWN_MAX):
            tail = jnp.where((lane6 >> 4) == s, pltpu.roll(slots[s], (16 * s + 64) % OBS, 1), tail)
        out_ref[HALF * 4 : HALF * 5, :] = tail


def split3(x):
    high = x.astype(bf16)
    rest = x - high.astype(f32)
    mid = rest.astype(bf16)
    return high, mid, (rest - mid.astype(f32)).astype(bf16)


def product_of_panel(factors, rows, panel):
    above, below = panel * WIDE, OBS - (panel + 1) * WIDE

    def placed(part):
        pieces = [part]
        if above:
            pieces.insert(0, jnp.zeros((above, OBS), bf16))
        if below:
            pieces.append(jnp.zeros((below, OBS), bf16))
        return jnp.concatenate(pieces, axis=0)

    high, mid, low = (placed(part) for part in split3(rows))
    right = jnp.concatenate([high, high, high, mid, mid, low], axis=0)
    return dot(factors, right)


def sweep(covariance, right, root, fill):
    blocks = OBS // 8
    deep = WIDE // 8
    left_rows = [covariance[8 * i : 8 * i + 8, :] for i in range(blocks)]
    right_rows = [right[8 * i : 8 * i + 8, :] for i in range(blocks)]
    root_rows = [root[8 * i : 8 * i + 8, :] for i in range(blocks)]
    sub = iota((8, OBS), 0)
    for panel in range(OBS // WIDE):
        own = range(deep * panel, deep * panel + deep)
        near = range(own.stop, min(own.stop + deep, blocks))
        base = WIDE * panel
        a = [left_rows[i] for i in own]
        b = [right_rows[i] for i in own]
        d = [root_rows[i] for i in own]
        columns = [[lane_of(a[h], base + r) for h in range(deep)] for r in range(WIDE)]
        high, mid, low = split3(jnp.concatenate(left_rows, axis=0))
        factors = jnp.concatenate([high, mid, low, high, mid, high], axis=1)
        scale = [jnp.ones((8, OBS), f32) for h in range(deep)]
        for j in range(WIDE):
            block, at = divmod(j, 8)
            at_j = sub == at
            pivot = sub_of(columns[j][block], at)
            inverse = 1.0 / pivot
            others = list(columns[j])
            others[block] = jnp.where(at_j, 0.0, others[block])
            factor = [other * inverse for other in others]
            if j + 1 < WIDE:
                row = sub_of(columns[j + 1][block], at)
                columns[j + 1] = [c - (o * row) * inverse for c, o in zip(columns[j + 1], others)]
            for r in range(j + 2, WIDE):
                row = sub_of(columns[r][block], at)
                columns[r] = [c - f * row for c, f in zip(columns[r], factor)]
            row = sub_of(a[block], at)
            a = [x - f * row for x, f in zip(a, factor)]
            weaker = 1.0 / (1.0 + sub_of(d[block], at) * lax.rsqrt(pivot))
            b[block] = b[block] * jnp.where(at_j, weaker, 1.0)
            row = sub_of(b[block], at)
            b = [x - f * row for x, f in zip(b, factor)]
            scale[block] = jnp.where(at_j, inverse, scale[block])
        a = [x * s for x, s in zip(a, scale)]
        b = [x * s for x, s in zip(b, scale)]
        for i in near:
            old = left_rows[i]
            for r in range(WIDE):
                factor = lane_of(old, base + r)
                left_rows[i] = left_rows[i] - factor * sub_of(a[r // 8], r % 8)
                right_rows[i] = right_rows[i] - factor * sub_of(b[r // 8], r % 8)
        far = [i for i in range(blocks) if i not in own and i not in near]
        change = product_of_panel(factors, jnp.concatenate(b, axis=0), panel)
        for i in far:
            right_rows[i] = right_rows[i] - change[8 * i : 8 * i + 8, :]
        if panel + 1 < OBS // WIDE:
            change = product_of_panel(factors, jnp.concatenate(a, axis=0), panel)
            for i in far:
                left_rows[i] = left_rows[i] - change[8 * i : 8 * i + 8, :]
        for h, i in enumerate(own):
            left_rows[i], right_rows[i] = a[h], b[h]
        for part in range(deep):
            fill(deep * panel + part)
    return jnp.concatenate(right_rows, axis=0)


def covariance_of(spread):
    high = spread.astype(bf16)
    rest = spread - high.astype(f32)
    mid = rest.astype(bf16)
    low = (rest - mid.astype(f32)).astype(bf16)
    small = dot_lanes(high, low) + dot_lanes(low, high) + dot_lanes(mid, mid)
    return dot_lanes(high, high) + (dot_lanes(high, mid) + dot_lanes(mid, high) + small)


def taper(rows_a, cols_a, rows_b, cols_b, circle):
    apart = jnp.abs(cols_a - cols_b)
    apart = jnp.minimum(apart, circle - apart)
    down = rows_a - rows_b
    return jnp.exp((apart * apart + down * down) * (-2.0 / (LON_DEV * LON_DEV)))


def pair_index(k, other):
    return k * (2 * BATCHES - 1 - k) // 2 + other - k - 1


def index_kernel(
    tiles,
    order_ref,
    place_ref,
    after_ref,
    table_ref,
    lists_ref,
    ens_ref,
    state_ref,
    pair_ref,
    local_ref,
    listed_ref,
    rank_ref,
    tile_col_ref,
    value_ref,
    root_ref,
    noise_ref,
    token_ref,
    raw_ref,
    turn_ref,
    turn2_ref,
    rows_ref,
    row_ref,
    col_ref,
    sem,
):
    circle = float(LON_DEV * tiles)
    pieces = CELL_DEV // OBS
    fetches = [
        pltpu.make_async_copy(ens_ref.at[:, OBS * c : OBS * c + OBS], raw_ref.at[c], sem.at[c])
        for c in range(pieces)
    ]
    for fetch in fetches:
        fetch.start()
    token_ref[...] = jnp.zeros((8, OBS), f32)
    listed_ref[BATCHES] = jnp.zeros((ROWS, OBS), f32)
    square = (OBS, OBS)
    lane = iota(square, 1)
    sub = iota(square, 0)
    lane_f = lane.astype(f32)
    turn_ref[...] = jnp.zeros(square, f32)
    turn2_ref[...] = jnp.full(square, float(OBS), f32)
    for k in range(BATCHES):
        b = order_ref[k]
        for part in range(3):
            turn_ref[16 * part + k : 16 * part + k + 1, :] = table_ref[pl.ds(BATCHES * part + b, 1), :]
        turn2_ref[k : k + 1, 0:ROUTE_CAP] = lists_ref[pl.ds(b, 1), :].astype(f32)
    turned = turn_ref[...].T
    listed = turn2_ref[...].T
    cells = turn_ref[0:16, :].astype(jnp.int32)
    rows_ref[0] = ((cells & (CELL_DEV - 1)) >> 4).astype(f32)
    rows_ref[1] = ((cells >> 10) * LON_DEV + (cells & 15)).astype(f32)
    rows_ref[2] = (cells >> 10).astype(f32)
    ones = jnp.ones(square, f32).astype(bf16)
    first_col = (place_ref[0] * LON_DEV).astype(f32)
    here = iota((ROWS, CELL_DEV), 1)
    here_row = (here >> 4).astype(f32)
    here_col = (here & 15).astype(f32) + first_col
    for k in range(BATCHES):
        cell = lane_of(turned, k).astype(jnp.int32)
        tile_col = (cell >> 10).astype(f32)
        row_ref[k] = ((cell & (CELL_DEV - 1)) >> 4).astype(f32)
        col_ref[k] = ((cell >> 10) * LON_DEV + (cell & 15)).astype(f32)
        tile_col_ref[k] = tile_col
        same = (tile_col == rows_ref[2, k : k + 1, :]) & (lane < sub)
        rank_ref[k] = dot(same.astype(f32).astype(bf16), ones)
        value_ref[k] = lane_of(turned, 16 + k)
        noise = lane_of(turned, 32 + k)
        noise_ref[k] = jnp.where(lane == sub, noise, 0.0)
        root_ref[k] = jnp.where(lane < MEM, jnp.sqrt(noise), 0.0)
        list_col = jnp.broadcast_to(listed[0:ROWS, k : k + 1], (ROWS, OBS))
        chosen = (list_col == lane_f[0:ROWS]).astype(f32)
        listed_ref[k] = chosen
        row_of = jnp.sum(chosen * rows_ref[0, k : k + 1, :], axis=1, keepdims=True)
        col_of = jnp.sum(chosen * rows_ref[1, k : k + 1, :], axis=1, keepdims=True)
        local_ref[k] = taper(row_of, col_of, here_row, here_col, circle) * (1.0 / (MEM - 1))

    def pairs(k, carry):
        source_row = rows_ref[0, pl.ds(k, 1), :]
        source_col = rows_ref[1, pl.ds(k, 1), :]
        source_tile = rows_ref[2, pl.ds(k, 1), :]

        def pair(other, carry):
            apart = jnp.abs(tile_col_ref[other] - source_tile)
            near = (apart <= 1.0) | (apart >= float(tiles - 1))
            weight = taper(row_ref[other], col_ref[other], source_row, source_col, circle)
            pair_ref[pair_index(k, other)] = jnp.where(near, weight * (1.0 / (MEM - 1)), 0.0)
            return carry

        return lax.fori_loop(k + 1, BATCHES, pair, carry)

    lax.fori_loop(0, BATCHES, pairs, 0)
    for fetch in fetches:
        fetch.wait()
    for c in range(pieces):
        for level in range(LEV_DEV):
            state_ref[level, :, OBS * c : OBS * c + OBS] = raw_ref[c, pl.ds(level, MEM, stride=LEV_DEV), :]


def serial_kernel(
    tiles,
    order_ref,
    place_ref,
    mine_ref,
    other_ref,
    token_ref,
    state_sent,
    pair_sent,
    local_sent,
    listed_sent,
    rank_sent,
    tile_col_sent,
    value_sent,
    root_sent,
    noise_sent,
    out_ref,
    state_ref,
    pair_ref,
    local_ref,
    listed_ref,
    rank_ref,
    tile_col_ref,
    value_ref,
    root_ref,
    noise_ref,
    raw_ref,
    paug_ref,
    past_ref,
    sem,
    sent_sem,
):
    moves = (
        (tile_col_sent, tile_col_ref),
        (rank_sent, rank_ref),
        (noise_sent, noise_ref),
        (value_sent, value_ref),
        (root_sent, root_ref),
        (listed_sent, listed_ref),
        (local_sent, local_ref),
        (pair_sent, pair_ref),
        (state_sent, state_ref),
    )
    fetches = [pltpu.make_async_copy(a, b, sent_sem.at[n]) for n, (a, b) in enumerate(moves)]
    for fetch in fetches:
        fetch.start()
    for fetch in fetches[:2]:
        fetch.wait()
    pieces = CELL_DEV // OBS
    square = (OBS, OBS)
    lane = iota(square, 1)
    lane_f = lane.astype(f32)
    is_member = lane < MEM
    group = lane >> 4
    fold = (lane == 64 + (iota(square, 0) & 15)).astype(f32).astype(bf16)
    lane_t = lane_f[:, 0:tiles]
    for k in range(BATCHES):
        b = order_ref[k]
        half = b // HALF
        here = b - half * HALF
        from_mine = half == place_ref[1]
        rank = rank_ref[k].astype(jnp.int32)
        chosen = (tile_col_ref[k, :, 0:tiles] == lane_t).astype(f32).astype(bf16)
        sent = []
        for r in range(5):
            rows = pl.ds(HALF * r + here, tiles, stride=PACK)
            sent.extend(split(jnp.where(from_mine, mine_ref[rows, :], other_ref[rows, :])))
        taken = dot(chosen, jnp.concatenate(sent, axis=1))
        parts = [taken[:, OBS * c : OBS * c + OBS] for c in range(10)]
        body = parts[0] + parts[1]
        for r in range(1, 4):
            body = jnp.where((rank & 3) == r, parts[2 * r] + parts[2 * r + 1], body)
        body = jnp.where(rank >= 4, pltpu.roll(body, 64, 1), body)
        at_rank = group == rank
        tail = dot(jnp.where(at_rank, parts[8], 0.0).astype(bf16), fold)
        tail = tail + dot(jnp.where(at_rank, parts[9], 0.0).astype(bf16), fold)
        gathered = jnp.where(lane < 64, body, tail)
        gathered = jnp.where(is_member, gathered, 0.0)
        mean = jnp.sum(gathered, axis=1, keepdims=True) * (1.0 / MEM)
        mean = jnp.broadcast_to(mean, square)
        paug_ref[k] = jnp.where(is_member, gathered - mean, jnp.where(lane == MEM, mean, 0.0))
    for fetch in fetches[2:]:
        fetch.wait()

    is_member_s = is_member[0:ROWS]
    lane_s = lane[0:ROWS]
    last_pair = pair_ref.shape[0] - 1
    for extra in range(BATCHES, 2 * BATCHES):
        paug_ref[extra] = jnp.zeros(square, f32)
    for part in range(4):
        past_ref[part] = jnp.zeros(square, bf16)

    def select():
        high, low, push_high, push_low = (past_ref[part] for part in range(4))
        chosen = listed_ref[BATCHES].astype(bf16)
        return dot(chosen, high), dot(chosen, low), dot(chosen, push_high) + dot(chosen, push_low)

    def operators(s_high, s_low, gain):
        moved = pltpu.roll(s_high, MEM, 1)
        first = jnp.where(is_member_s, s_high, moved)
        second = jnp.where(lane_s < 2 * MEM - OBS, moved, pltpu.roll(s_low, 2 * MEM - OBS, 1))
        left = jnp.concatenate([first, second], axis=1).astype(bf16)
        gain = jnp.where(is_member_s, gain + lane_of(gain, MEM), 0.0)
        gain_high = gain.astype(bf16).astype(f32)
        stacked = jnp.concatenate([gain_high, gain_high, gain - gain_high, jnp.zeros_like(gain)], axis=0)
        return left, stacked.T[0:MEM, :].astype(bf16)

    def crossed_level(level, before, left):
        x_high, x_low = split(state_ref[level])
        filler = jnp.zeros((16, CELL_DEV), bf16)
        crossed = dot(left, jnp.concatenate([x_high, x_low, x_high, filler], axis=0))
        t_high, t_low = split(crossed * local_ref[before])
        filler = jnp.zeros((ROWS, CELL_DEV), bf16)
        return jnp.concatenate([t_high, t_low, t_high, filler], axis=0)

    def renew_level(level, mixing, tapered):
        state_ref[level] = state_ref[level] + dot(mixing, tapered)

    def tapered_by(upcoming, high, low, pair):
        up_high, up_low = split(jnp.where(is_member, upcoming, 0.0))
        crossed = dot_lanes(up_high, high) + dot_lanes(up_low, high) + dot_lanes(up_high, low)
        return split(crossed * pair_ref[jnp.clip(pair, 0, last_pair)])

    def pushed(parts, push_high, push_low):
        t_high, t_low = parts
        return dot(t_high, push_high) + dot(t_low, push_high) + dot(t_high, push_low)

    def turn(k, slots):
        before = jnp.maximum(k - 1, 0)
        now = paug_ref[k]
        spread = jnp.where(is_member, now, 0.0)
        high, low = split(spread)
        old_high, old_low, old_push_high, old_push_low = (past_ref[part] for part in range(4))
        covariance = covariance_of(spread) * (1.0 / (MEM - 1)) + noise_ref[k]
        right = jnp.where(is_member, now, jnp.where(lane == MEM, value_ref[k] - now, 0.0))
        waiting = []
        made = {}

        def finish_slot(slot, other, parts):
            upcoming = paug_ref[other] + pushed(parts, old_push_high, old_push_low)
            if slot == 0:
                made["next"] = upcoming

                def taper_next():
                    made["tapered"] = tapered_by(upcoming, high, low, pair_index(k, other))

                waiting.append(taper_next)
            else:
                paug_ref[other] = upcoming

        def fill(p):
            ready = waiting[:-LAG] if p < OBS // 8 - 1 else waiting[:]
            del waiting[: len(ready)]
            for finish in ready:
                finish()
            if p == 0:
                made["selected"] = select()
            if p == 1:
                made["operators"] = operators(*made["selected"])
            if p < slots:
                other = k + 1 + p
                parts = tapered_by(paug_ref[other], old_high, old_low, pair_index(k - 1, other))
                waiting.append(lambda: finish_slot(p, other, parts))
            if p in LEVEL_TURNS:
                level = LEVEL_TURNS.index(p)
                left, mixing = made["operators"]
                tapered = crossed_level(level, before, left)
                waiting.append(lambda: renew_level(level, mixing, tapered))

        solved = sweep(covariance, right, root_ref[k], fill)
        push = jnp.where(is_member, -solved, solved)
        push_high, push_low = split(push)
        paug_ref[k + 1] = made["next"] + pushed(made["tapered"], push_high, push_low)
        for finish in waiting:
            finish()
        for part, value in enumerate((high, low, push_high, push_low)):
            past_ref[part] = value
        listed_ref[BATCHES] = listed_ref[k]

    for start in range(0, BATCHES, SEGMENT):

        def step(k, carry):
            turn(k, BATCHES - 1 - start)
            return carry

        lax.fori_loop(start, start + SEGMENT, step, 0)
    left, mixing = operators(*select())
    tapered = [crossed_level(level, BATCHES - 1, left) for level in range(LEV_DEV)]
    for level in range(LEV_DEV):
        renew_level(level, mixing, tapered[level])
    stores = [
        pltpu.make_async_copy(raw_ref.at[c], out_ref.at[:, OBS * c : OBS * c + OBS], sem.at[c])
        for c in range(pieces)
    ]
    for c in range(pieces):
        for level in range(LEV_DEV):
            raw_ref[c, pl.ds(level, MEM, stride=LEV_DEV), :] = state_ref[level, :, OBS * c : OBS * c + OBS]
        stores[c].start()
    for store in stores:
        store.wait()


def whole(space):
    return pl.BlockSpec(memory_space=space)


def body(ensemble, obs_cell, obs_value, obs_noise, obs_weight, tile_lists, batch_order):
    tiles = lax.axis_size(LON)
    place = jnp.stack([lax.axis_index(LON), lax.axis_index("lev")]).astype(jnp.int32)
    mine = jnp.concatenate([obs_cell.astype(f32), obs_value, obs_noise], axis=0)
    table = sent_to_all(mine, LON)
    table = jnp.moveaxis(table, 0, 1).reshape(3 * BATCHES, OBS)
    flat = ensemble.reshape(MEM * LEV_DEV, CELL_DEV)
    packed = jax.ShapeDtypeStruct((PACK, OBS), f32)
    keep, send = pl.pallas_call(
        probe_kernel,
        name="probe_kernel",
        out_shape=(packed, packed),
        in_specs=[whole(pltpu.SMEM), whole(pl.ANY), whole(pltpu.VMEM), whole(pltpu.VMEM)],
        out_specs=(whole(pltpu.VMEM), whole(pltpu.VMEM)),
        scratch_shapes=[
            pltpu.VMEM((OBS, OBS), f32),
            pltpu.VMEM(flat.shape, f32),
            pltpu.SemaphoreType.DMA,
        ],
        compiler_params=pltpu.CompilerParams(vmem_limit_bytes=62 << 20),
    )(place, flat, table, obs_weight)
    swap = [(0, 1), (1, 0)]
    portion = keep + lax.ppermute(send, "lev", swap)
    mine = sent_to_all(portion, LON)
    square = (BATCHES, OBS, OBS)
    pair_count = BATCHES * (BATCHES - 1) // 2
    state_shape = (LEV_DEV, MEM, CELL_DEV)
    raw_shape = (CELL_DEV // OBS, MEM * LEV_DEV, OBS)

    def index_run(*refs):
        given, sent, token, held, rest = refs[:6], refs[6:15], refs[15], refs[16:25], refs[25:]
        index_kernel(tiles, *given, *held, token, *rest[:-1])
        copies = [pltpu.make_async_copy(a, b, rest[-1].at[n]) for n, (a, b) in enumerate(zip(held, sent))]
        for copy in copies:
            copy.start()
        for copy in copies:
            copy.wait()

    shapes = (
        state_shape,
        (pair_count, OBS, OBS),
        (BATCHES, ROWS, CELL_DEV),
        (BATCHES + 1, ROWS, OBS),
        square,
        square,
        square,
        square,
        square,
        (8, OBS),
    )
    known = pl.pallas_call(
        index_run,
        name="index_kernel",
        out_shape=tuple(jax.ShapeDtypeStruct(shape, f32) for shape in shapes),
        in_specs=[whole(pltpu.SMEM)] * 2 + [whole(pltpu.VMEM)] * 3 + [whole(pl.ANY)],
        out_specs=tuple(whole(pltpu.HBM) for shape in shapes[:-1]) + (whole(pltpu.VMEM),),
        scratch_shapes=[pltpu.VMEM(shape, f32) for shape in shapes[:-1]]
        + [
            pltpu.VMEM(raw_shape, f32),
            pltpu.VMEM((OBS, OBS), f32),
            pltpu.VMEM((OBS, OBS), f32),
            pltpu.VMEM((3, 16, OBS), f32),
            pltpu.VMEM(square, f32),
            pltpu.VMEM(square, f32),
            pltpu.SemaphoreType.DMA((CELL_DEV // OBS,)),
            pltpu.SemaphoreType.DMA((len(shapes) - 1,)),
        ],
        cost_estimate=pl.CostEstimate(flops=40 << 20, transcendentals=2 << 20, bytes_accessed=16 << 20),
        compiler_params=pltpu.CompilerParams(vmem_limit_bytes=62 << 20),
    )(batch_order, place, portion, table, tile_lists, flat)
    mine, token = lax.optimization_barrier((mine, known[-1]))
    known = (*known[:-1], token)
    other = lax.ppermute(mine, "lev", swap)
    mine = mine.reshape(tiles * PACK, OBS)
    other = other.reshape(tiles * PACK, OBS)

    def run(*refs):
        serial_kernel(tiles, *refs)

    result = pl.pallas_call(
        run,
        name="serial_kernel",
        out_shape=jax.ShapeDtypeStruct(flat.shape, f32),
        in_specs=[whole(pltpu.SMEM)] * 2
        + [whole(pltpu.VMEM)] * 3
        + [whole(pltpu.HBM)] * 9,
        out_specs=whole(pl.ANY),
        scratch_shapes=[pltpu.VMEM(shape, f32) for shape in shapes[:-1]]
        + [
            pltpu.VMEM(raw_shape, f32),
            pltpu.VMEM((2 * BATCHES, OBS, OBS), f32),
            pltpu.VMEM((4, OBS, OBS), bf16),
            pltpu.SemaphoreType.DMA((CELL_DEV // OBS,)),
            pltpu.SemaphoreType.DMA((len(shapes) - 1,)),
        ],
        compiler_params=pltpu.CompilerParams(vmem_limit_bytes=60 << 20),
    )(batch_order, place, mine, other, known[-1], *known[:-1])
    return result.reshape(MEM, LEV_DEV, CELL_DEV)


def solution(mesh):
    finer = Mesh(
        mesh.devices.reshape(4, 4, 4, mesh.shape["lev"]), ("lon_0", "lon_1", "lon_2", "lev")
    )
    in_specs = (
        P(None, "lev", LON),
        P(None, LON),
        P(None, LON),
        P(None, LON),
        P(None, "lev", None),
        P(None, LON),
        P(),
    )
    out_specs = P(None, "lev", LON)
    return jax.shard_map(body, mesh=finer, in_specs=in_specs, out_specs=out_specs, check_vma=False)
```

```python
import jax
import jax.numpy as jnp
from jax import lax
from jax.experimental import pallas as pl
from jax.experimental.pallas import tpu as pltpu
from jax.sharding import Mesh
from jax.sharding import PartitionSpec as P

MEM = 80
OBS = 128
ROUTE_CAP = 24
OWN_MAX = 8
LON_DEV = 16
CELL_DEV = 1024
BATCHES = 12
LEV_DEV = 8
ROWS = 32
HALF = 6
PACK = 32
SEGMENT = 4
LAG = 3
CHUNKS = 4
WIDE = 16
LEVEL_TURNS = (2, 4, 6, 8, 10, 11, 12, 13)
LON = ("lon_0", "lon_1", "lon_2")
f32 = jnp.float32
bf16 = jnp.bfloat16


def sent_to_all(array, axis):
    copies = jnp.broadcast_to(array, (lax.axis_size(axis), *array.shape))
    return lax.all_to_all(copies, axis, split_axis=0, concat_axis=0, tiled=True)


def iota(shape, dim):
    return lax.broadcasted_iota(jnp.int32, shape, dim)


def split(x):
    high = x.astype(bf16)
    return high, (x - high.astype(f32)).astype(bf16)


def dot(a, b):
    return jnp.dot(a, b, preferred_element_type=f32)


def dot_lanes(a, b):
    return lax.dot_general(a, b, (((1,), (1,)), ((), ())), preferred_element_type=f32)


def lane_of(x, lane):
    return jnp.broadcast_to(x[:, lane : lane + 1], x.shape)


def sub_of(x, row):
    return jnp.broadcast_to(x[row : row + 1, :], x.shape)


def probe_kernel(place_ref, ens_ref, table_ref, weight_ref, keep_ref, send_ref, turn_ref, block_ref, sem):
    tile, level_half = place_ref[0], place_ref[1]
    width = CELL_DEV // CHUNKS
    fetches = [
        pltpu.make_async_copy(ens_ref.at[:, width * c : width * c + width], block_ref.at[c], sem.at[c])
        for c in range(CHUNKS)
    ]
    for fetch in fetches:
        fetch.start()
    cells = table_ref[0:16, :].astype(jnp.int32)
    own = (cells >> 10) == tile
    lane = iota((OBS, OBS), 1)
    sub = iota((OBS, OBS), 0)
    before = (sub < lane).astype(f32).astype(bf16)
    rank = dot(own.astype(f32).astype(bf16), before)
    slot = jnp.where(own, iota((16, OBS), 0).astype(f32) * OWN_MAX + rank, -1.0)
    turn_ref[...] = jnp.zeros((OBS, OBS), f32)
    turn_ref[0:16, :] = slot
    slot_turned = turn_ref[...].T
    within = cells & (CELL_DEV - 1)
    row = (within >> 4).astype(f32)
    col = (within & 15).astype(f32)
    lane_f = lane.astype(f32)
    sub8 = iota((8, OBS), 0)
    picked = jnp.zeros((32, OBS), f32)
    for b in range(BATCHES):
        chosen = (lane_of(slot_turned, b) == lane_f).astype(f32).astype(bf16)
        weight = weight_ref[b]
        w_high = weight.astype(bf16).astype(f32)
        w_rest = weight - w_high
        w_mid = w_rest.astype(bf16).astype(f32)
        place = jnp.where(
            sub8 == 0,
            jnp.broadcast_to(row[b : b + 1, :], (8, OBS)),
            jnp.where(sub8 == 1, jnp.broadcast_to(col[b : b + 1, :], (8, OBS)), 0.0),
        )
        left = jnp.concatenate([place, w_high, w_mid, w_rest - w_mid], axis=0).astype(bf16)
        picked = picked + dot(left, chosen)
    cell = picked[0:1, :] * LON_DEV + picked[1:2, :]
    weight = picked[8:16, :] + picked[16:24, :] + picked[24:32, :]
    column = iota((width, OBS), 0).astype(f32)
    taken = jnp.zeros((MEM * LEV_DEV, OBS), f32)
    for c in range(CHUNKS):
        one_hot = (column + float(width * c) == cell).astype(f32).astype(bf16)
        fetches[c].wait()
        high, low = split(block_ref[c])
        taken = taken + (dot(high, one_hot) + dot(low, one_hot))
    summed = jnp.sum(taken.reshape(MEM, LEV_DEV, OBS) * weight[None], axis=1)
    turn_ref[...] = jnp.zeros((OBS, OBS), f32)
    turn_ref[0:MEM, :] = summed
    turn_ref[...] = turn_ref[...].T
    lane6 = iota((HALF, OBS), 1)
    for half, out_ref in ((level_half, keep_ref), (1 - level_half, send_ref)):
        first = half * (HALF * OWN_MAX)
        slots = [turn_ref[pl.ds(first + s, HALF, stride=OWN_MAX), :] for s in range(OWN_MAX)]
        out_ref[...] = jnp.zeros((PACK, OBS), f32)
        tail = jnp.zeros((HALF, OBS), f32)
        for r in range(4):
            both = jnp.where(lane6 < 64, slots[r], pltpu.roll(slots[r + 4], 64, 1))
            out_ref[HALF * r : HALF * r + HALF, :] = both
        for s in range(OWN_MAX):
            tail = jnp.where((lane6 >> 4) == s, pltpu.roll(slots[s], (16 * s + 64) % OBS, 1), tail)
        out_ref[HALF * 4 : HALF * 5, :] = tail


def split3(x):
    high = x.astype(bf16)
    rest = x - high.astype(f32)
    mid = rest.astype(bf16)
    return high, mid, (rest - mid.astype(f32)).astype(bf16)


def product_of_panel(factors, rows, panel):
    above, below = panel * WIDE, OBS - (panel + 1) * WIDE

    def placed(part):
        pieces = [part]
        if above:
            pieces.insert(0, jnp.zeros((above, OBS), bf16))
        if below:
            pieces.append(jnp.zeros((below, OBS), bf16))
        return jnp.concatenate(pieces, axis=0)

    high, mid, low = (placed(part) for part in split3(rows))
    right = jnp.concatenate([high, high, high, mid, mid, low], axis=0)
    return dot(factors, right)


def added(terms):
    while len(terms) > 1:
        terms = [x + y for x, y in zip(terms[::2], terms[1::2])]
    return terms[0]


def sweep(covariance, right, root, fill):
    blocks = OBS // 8
    deep = WIDE // 8
    left_rows = [covariance[8 * i : 8 * i + 8, :] for i in range(blocks)]
    right_rows = [right[8 * i : 8 * i + 8, :] for i in range(blocks)]
    root_rows = [root[8 * i : 8 * i + 8, :] for i in range(blocks)]
    sub = iota((8, OBS), 0)
    for panel in range(OBS // WIDE):
        own = range(deep * panel, deep * panel + deep)
        near = range(own.stop, min(own.stop + deep, blocks))
        base = WIDE * panel
        a = [left_rows[i] for i in own]
        b = [right_rows[i] for i in own]
        d = [root_rows[i] for i in own]
        columns = [[lane_of(a[h], base + r) for h in range(deep)] for r in range(WIDE)]
        high, mid, low = split3(jnp.concatenate(left_rows, axis=0))
        factors = jnp.concatenate([high, mid, low, high, mid, high], axis=1)
        scale = [jnp.ones((8, OBS), f32) for h in range(deep)]
        for j in range(WIDE):
            block, at = divmod(j, 8)
            at_j = sub == at
            pivot = sub_of(columns[j][block], at)
            if j % 2 == 0:
                inverse = 1.0 / pivot
                beside = sub_of(columns[j + 1][block], at)
                corner = sub_of(columns[j + 1][block], at + 1)
                inverse_next = pivot / (pivot * corner - beside * beside)
            else:
                inverse = inverse_next
            others = list(columns[j])
            others[block] = jnp.where(at_j, 0.0, others[block])
            factor = [other * inverse for other in others]
            if j + 1 < WIDE:
                row = sub_of(columns[j + 1][block], at)
                columns[j + 1] = [c - (o * row) * inverse for c, o in zip(columns[j + 1], others)]
            for r in range(j + 2, WIDE):
                row = sub_of(columns[r][block], at)
                columns[r] = [c - f * row for c, f in zip(columns[r], factor)]
            row = sub_of(a[block], at)
            a = [x - f * row for x, f in zip(a, factor)]
            weaker = 1.0 / (1.0 + sub_of(d[block], at) * lax.rsqrt(pivot))
            b[block] = b[block] * jnp.where(at_j, weaker, 1.0)
            row = sub_of(b[block], at)
            b = [x - f * row for x, f in zip(b, factor)]
            scale[block] = jnp.where(at_j, inverse, scale[block])
        a = [x * s for x, s in zip(a, scale)]
        b = [x * s for x, s in zip(b, scale)]
        for i in near:
            factor = [lane_of(left_rows[i], base + r) for r in range(WIDE)]
            left_rows[i] = left_rows[i] - added([factor[r] * sub_of(a[r // 8], r % 8) for r in range(WIDE)])
            right_rows[i] = right_rows[i] - added([factor[r] * sub_of(b[r // 8], r % 8) for r in range(WIDE)])
        far = [i for i in range(blocks) if i not in own and i not in near]
        change = product_of_panel(factors, jnp.concatenate(b, axis=0), panel)
        for i in far:
            right_rows[i] = right_rows[i] - change[8 * i : 8 * i + 8, :]
        if panel + 1 < OBS // WIDE:
            change = product_of_panel(factors, jnp.concatenate(a, axis=0), panel)
            for i in far:
                left_rows[i] = left_rows[i] - change[8 * i : 8 * i + 8, :]
        for h, i in enumerate(own):
            left_rows[i], right_rows[i] = a[h], b[h]
        for part in range(deep):
            fill(deep * panel + part)
    return jnp.concatenate(right_rows, axis=0)


def covariance_of(spread):
    high = spread.astype(bf16)
    rest = spread - high.astype(f32)
    mid = rest.astype(bf16)
    low = (rest - mid.astype(f32)).astype(bf16)
    small = dot_lanes(high, low) + dot_lanes(low, high) + dot_lanes(mid, mid)
    return dot_lanes(high, high) + (dot_lanes(high, mid) + dot_lanes(mid, high) + small)


def taper(rows_a, cols_a, rows_b, cols_b, circle):
    apart = jnp.abs(cols_a - cols_b)
    apart = jnp.minimum(apart, circle - apart)
    down = rows_a - rows_b
    return jnp.exp((apart * apart + down * down) * (-2.0 / (LON_DEV * LON_DEV)))


def pair_index(k, other):
    return k * (2 * BATCHES - 1 - k) // 2 + other - k - 1


def index_kernel(
    tiles,
    order_ref,
    place_ref,
    after_ref,
    table_ref,
    lists_ref,
    ens_ref,
    state_ref,
    pair_ref,
    local_ref,
    listed_ref,
    rank_ref,
    tile_col_ref,
    value_ref,
    root_ref,
    noise_ref,
    token_ref,
    raw_ref,
    turn_ref,
    turn2_ref,
    rows_ref,
    row_ref,
    col_ref,
    sem,
):
    circle = float(LON_DEV * tiles)
    pieces = CELL_DEV // OBS
    fetches = [
        pltpu.make_async_copy(ens_ref.at[:, OBS * c : OBS * c + OBS], raw_ref.at[c], sem.at[c])
        for c in range(pieces)
    ]
    for fetch in fetches:
        fetch.start()
    token_ref[...] = jnp.zeros((8, OBS), f32)
    listed_ref[BATCHES] = jnp.zeros((ROWS, OBS), f32)
    square = (OBS, OBS)
    lane = iota(square, 1)
    sub = iota(square, 0)
    lane_f = lane.astype(f32)
    turn_ref[...] = jnp.zeros(square, f32)
    turn2_ref[...] = jnp.full(square, float(OBS), f32)
    for k in range(BATCHES):
        b = order_ref[k]
        for part in range(3):
            turn_ref[16 * part + k : 16 * part + k + 1, :] = table_ref[pl.ds(BATCHES * part + b, 1), :]
        turn2_ref[k : k + 1, 0:ROUTE_CAP] = lists_ref[pl.ds(b, 1), :].astype(f32)
    turned = turn_ref[...].T
    listed = turn2_ref[...].T
    cells = turn_ref[0:16, :].astype(jnp.int32)
    rows_ref[0] = ((cells & (CELL_DEV - 1)) >> 4).astype(f32)
    rows_ref[1] = ((cells >> 10) * LON_DEV + (cells & 15)).astype(f32)
    rows_ref[2] = (cells >> 10).astype(f32)
    ones = jnp.ones(square, f32).astype(bf16)
    first_col = (place_ref[0] * LON_DEV).astype(f32)
    here = iota((ROWS, CELL_DEV), 1)
    here_row = (here >> 4).astype(f32)
    here_col = (here & 15).astype(f32) + first_col
    for k in range(BATCHES):
        cell = lane_of(turned, k).astype(jnp.int32)
        tile_col = (cell >> 10).astype(f32)
        row_ref[k] = ((cell & (CELL_DEV - 1)) >> 4).astype(f32)
        col_ref[k] = ((cell >> 10) * LON_DEV + (cell & 15)).astype(f32)
        tile_col_ref[k] = tile_col
        same = (tile_col == rows_ref[2, k : k + 1, :]) & (lane < sub)
        rank_ref[k] = dot(same.astype(f32).astype(bf16), ones)
        value_ref[k] = lane_of(turned, 16 + k)
        noise = lane_of(turned, 32 + k)
        noise_ref[k] = jnp.where(lane == sub, noise, 0.0)
        root_ref[k] = jnp.where(lane < MEM, jnp.sqrt(noise), 0.0)
        list_col = jnp.broadcast_to(listed[0:ROWS, k : k + 1], (ROWS, OBS))
        chosen = (list_col == lane_f[0:ROWS]).astype(f32)
        listed_ref[k] = chosen
        row_of = jnp.sum(chosen * rows_ref[0, k : k + 1, :], axis=1, keepdims=True)
        col_of = jnp.sum(chosen * rows_ref[1, k : k + 1, :], axis=1, keepdims=True)
        local_ref[k] = taper(row_of, col_of, here_row, here_col, circle) * (1.0 / (MEM - 1))

    def pairs(k, carry):
        source_row = rows_ref[0, pl.ds(k, 1), :]
        source_col = rows_ref[1, pl.ds(k, 1), :]
        source_tile = rows_ref[2, pl.ds(k, 1), :]

        def pair(other, carry):
            apart = jnp.abs(tile_col_ref[other] - source_tile)
            near = (apart <= 1.0) | (apart >= float(tiles - 1))
            weight = taper(row_ref[other], col_ref[other], source_row, source_col, circle)
            pair_ref[pair_index(k, other)] = jnp.where(near, weight * (1.0 / (MEM - 1)), 0.0)
            return carry

        return lax.fori_loop(k + 1, BATCHES, pair, carry)

    lax.fori_loop(0, BATCHES, pairs, 0)
    for fetch in fetches:
        fetch.wait()
    for c in range(pieces):
        for level in range(LEV_DEV):
            state_ref[level, :, OBS * c : OBS * c + OBS] = raw_ref[c, pl.ds(level, MEM, stride=LEV_DEV), :]


def serial_kernel(
    tiles,
    order_ref,
    place_ref,
    mine_ref,
    other_ref,
    token_ref,
    state_sent,
    pair_sent,
    local_sent,
    listed_sent,
    rank_sent,
    tile_col_sent,
    value_sent,
    root_sent,
    noise_sent,
    out_ref,
    state_ref,
    pair_ref,
    local_ref,
    listed_ref,
    rank_ref,
    tile_col_ref,
    value_ref,
    root_ref,
    noise_ref,
    raw_ref,
    paug_ref,
    past_ref,
    soon_ref,
    sem,
    sent_sem,
):
    moves = (
        (tile_col_sent, tile_col_ref),
        (rank_sent, rank_ref),
        (noise_sent, noise_ref),
        (value_sent, value_ref),
        (root_sent, root_ref),
        (listed_sent, listed_ref),
        (local_sent, local_ref),
        (pair_sent, pair_ref),
        (state_sent, state_ref),
    )
    first_pair = pltpu.make_async_copy(pair_sent.at[0:1], soon_ref, sem.at[0])
    first_pair.start()
    fetches = [pltpu.make_async_copy(a, b, sent_sem.at[n]) for n, (a, b) in enumerate(moves)]
    for fetch in fetches:
        fetch.start()
    for fetch in fetches[:2]:
        fetch.wait()
    square = (OBS, OBS)
    lane = iota(square, 1)
    lane_f = lane.astype(f32)
    is_member = lane < MEM
    group = lane >> 4
    fold = (lane == 64 + (iota(square, 0) & 15)).astype(f32).astype(bf16)
    lane_t = lane_f[:, 0:tiles]
    for k in range(BATCHES):
        b = order_ref[k]
        half = b // HALF
        here = b - half * HALF
        from_mine = half == place_ref[1]
        rank = rank_ref[k].astype(jnp.int32)
        chosen = (tile_col_ref[k, :, 0:tiles] == lane_t).astype(f32).astype(bf16)
        sent = []
        for r in range(5):
            rows = pl.ds(HALF * r + here, tiles, stride=PACK)
            sent.extend(split(jnp.where(from_mine, mine_ref[rows, :], other_ref[rows, :])))
        taken = dot(chosen, jnp.concatenate(sent, axis=1))
        parts = [taken[:, OBS * c : OBS * c + OBS] for c in range(10)]
        body = parts[0] + parts[1]
        for r in range(1, 4):
            body = jnp.where((rank & 3) == r, parts[2 * r] + parts[2 * r + 1], body)
        body = jnp.where(rank >= 4, pltpu.roll(body, 64, 1), body)
        at_rank = group == rank
        tail = dot(jnp.where(at_rank, parts[8], 0.0).astype(bf16), fold)
        tail = tail + dot(jnp.where(at_rank, parts[9], 0.0).astype(bf16), fold)
        gathered = jnp.where(lane < 64, body, tail)
        gathered = jnp.where(is_member, gathered, 0.0)
        mean = jnp.sum(gathered, axis=1, keepdims=True) * (1.0 / MEM)
        mean = jnp.broadcast_to(mean, square)
        paug_ref[k] = jnp.where(is_member, gathered - mean, jnp.where(lane == MEM, mean, 0.0))
    for fetch in fetches[2:6]:
        fetch.wait()
    first_pair.wait()

    is_member_s = is_member[0:ROWS]
    lane_s = lane[0:ROWS]
    last_pair = pair_ref.shape[0] - 1
    for extra in range(BATCHES, 2 * BATCHES):
        paug_ref[extra] = jnp.zeros(square, f32)
    for part in range(4):
        past_ref[part] = jnp.zeros(square, bf16)

    def select():
        high, low, push_high, push_low = (past_ref[part] for part in range(4))
        chosen = listed_ref[BATCHES].astype(bf16)
        return dot(chosen, high), dot(chosen, low), dot(chosen, push_high) + dot(chosen, push_low)

    def operators(s_high, s_low, gain):
        moved = pltpu.roll(s_high, MEM, 1)
        first = jnp.where(is_member_s, s_high, moved)
        second = jnp.where(lane_s < 2 * MEM - OBS, moved, pltpu.roll(s_low, 2 * MEM - OBS, 1))
        left = jnp.concatenate([first, second], axis=1).astype(bf16)
        gain = jnp.where(is_member_s, gain + lane_of(gain, MEM), 0.0)
        gain_high = gain.astype(bf16).astype(f32)
        stacked = jnp.concatenate([gain_high, gain_high, gain - gain_high, jnp.zeros_like(gain)], axis=0)
        return left, stacked.T[0:MEM, :].astype(bf16)

    def crossed_level(level, before, left, part=slice(0, CELL_DEV)):
        width = part.stop - part.start
        x_high, x_low = split(state_ref[level, :, part])
        filler = jnp.zeros((16, width), bf16)
        crossed = dot(left, jnp.concatenate([x_high, x_low, x_high, filler], axis=0))
        t_high, t_low = split(crossed * local_ref[before, :, part])
        filler = jnp.zeros((ROWS, width), bf16)
        return jnp.concatenate([t_high, t_low, t_high, filler], axis=0)

    def renew_level(level, mixing, tapered):
        state_ref[level] = state_ref[level] + dot(mixing, tapered)

    def pair_weight(pair):
        return pair_ref[jnp.clip(pair, 0, last_pair)]

    def tapered_by(upcoming, high, low, weight):
        up_high, up_low = split(jnp.where(is_member, upcoming, 0.0))
        crossed = dot_lanes(up_high, high) + dot_lanes(up_low, high) + dot_lanes(up_high, low)
        return split(crossed * weight)

    def pushed(parts, push_high, push_low):
        t_high, t_low = parts
        return dot(t_high, push_high) + dot(t_low, push_high) + dot(t_high, push_low)

    def turn(k, slots):
        before = jnp.maximum(k - 1, 0)
        now = paug_ref[k]
        spread = jnp.where(is_member, now, 0.0)
        high, low = split(spread)
        old_high, old_low, old_push_high, old_push_low = (past_ref[part] for part in range(4))
        covariance = covariance_of(spread) * (1.0 / (MEM - 1)) + noise_ref[k]
        right = jnp.where(is_member, now, jnp.where(lane == MEM, value_ref[k] - now, 0.0))
        waiting = []
        made = {}

        def finish_slot(slot, other, parts):
            upcoming = paug_ref[other] + pushed(parts, old_push_high, old_push_low)
            if slot == 0:
                made["next"] = upcoming

                def taper_next():
                    made["tapered"] = tapered_by(upcoming, high, low, pair_weight(pair_index(k, other)))

                waiting.append(taper_next)
            else:
                paug_ref[other] = upcoming

        def fill(p):
            if slots is None:
                if p == 0:
                    made["next"] = paug_ref[1]
                    made["tapered"] = tapered_by(made["next"], high, low, soon_ref[0])
                return
            ready = waiting[:-LAG] if p < OBS // 8 - 1 else waiting[:]
            del waiting[: len(ready)]
            for finish in ready:
                finish()
            if p == 0:
                made["selected"] = select()
            if p == 1:
                made["operators"] = operators(*made["selected"])
            if p < slots:
                other = k + 1 + p
                parts = tapered_by(paug_ref[other], old_high, old_low, pair_weight(pair_index(k - 1, other)))
                waiting.append(lambda: finish_slot(p, other, parts))
            if p in LEVEL_TURNS:
                level = LEVEL_TURNS.index(p)
                left, mixing = made["operators"]
                tapered = crossed_level(level, before, left)
                waiting.append(lambda: renew_level(level, mixing, tapered))

        solved = sweep(covariance, right, root_ref[k], fill)
        push = jnp.where(is_member, -solved, solved)
        push_high, push_low = split(push)
        paug_ref[k + 1] = made["next"] + pushed(made["tapered"], push_high, push_low)
        for finish in waiting:
            finish()
        for part, value in enumerate((high, low, push_high, push_low)):
            past_ref[part] = value
        listed_ref[BATCHES] = listed_ref[k]

    turn(0, None)
    for fetch in fetches[6:]:
        fetch.wait()
    for start in range(0, BATCHES, SEGMENT):
        begin = max(start, 1)

        def step(k, carry):
            turn(k, BATCHES - 1 - begin)
            return carry

        lax.fori_loop(begin, start + SEGMENT, step, 0)
    left, mixing = operators(*select())
    pieces = CELL_DEV // OBS
    stores = [
        pltpu.make_async_copy(raw_ref.at[c], out_ref.at[:, OBS * c : OBS * c + OBS], sem.at[c])
        for c in range(pieces)
    ]
    for c in range(0, pieces, 2):
        part = slice(OBS * c, OBS * c + 2 * OBS)
        tapered = [crossed_level(level, BATCHES - 1, left, part) for level in range(LEV_DEV)]
        for level in range(LEV_DEV):
            block = state_ref[level, :, part] + dot(mixing, tapered[level])
            rows = pl.ds(level, MEM, stride=LEV_DEV)
            raw_ref[c, rows, :] = block[:, 0:OBS]
            raw_ref[c + 1, rows, :] = block[:, OBS : 2 * OBS]
        stores[c].start()
        stores[c + 1].start()
    for store in stores:
        store.wait()


def whole(space):
    return pl.BlockSpec(memory_space=space)


def body(ensemble, obs_cell, obs_value, obs_noise, obs_weight, tile_lists, batch_order):
    tiles = lax.axis_size(LON)
    place = jnp.stack([lax.axis_index(LON), lax.axis_index("lev")]).astype(jnp.int32)
    mine = jnp.concatenate([obs_cell.astype(f32), obs_value, obs_noise], axis=0)
    table = sent_to_all(mine, LON)
    table = jnp.moveaxis(table, 0, 1).reshape(3 * BATCHES, OBS)
    flat = ensemble.reshape(MEM * LEV_DEV, CELL_DEV)
    packed = jax.ShapeDtypeStruct((PACK, OBS), f32)
    keep, send = pl.pallas_call(
        probe_kernel,
        name="probe_kernel",
        out_shape=(packed, packed),
        in_specs=[whole(pltpu.SMEM), whole(pl.ANY), whole(pltpu.VMEM), whole(pltpu.VMEM)],
        out_specs=(whole(pltpu.VMEM), whole(pltpu.VMEM)),
        scratch_shapes=[
            pltpu.VMEM((OBS, OBS), f32),
            pltpu.VMEM((CHUNKS, MEM * LEV_DEV, CELL_DEV // CHUNKS), f32),
            pltpu.SemaphoreType.DMA((CHUNKS,)),
        ],
        compiler_params=pltpu.CompilerParams(vmem_limit_bytes=62 << 20),
    )(place, flat, table, obs_weight)
    swap = [(0, 1), (1, 0)]
    portion = keep + lax.ppermute(send, "lev", swap)
    mine = sent_to_all(portion, LON)
    square = (BATCHES, OBS, OBS)
    pair_count = BATCHES * (BATCHES - 1) // 2
    state_shape = (LEV_DEV, MEM, CELL_DEV)
    raw_shape = (CELL_DEV // OBS, MEM * LEV_DEV, OBS)

    def index_run(*refs):
        given, sent, token, held, rest = refs[:6], refs[6:15], refs[15], refs[16:25], refs[25:]
        index_kernel(tiles, *given, *held, token, *rest[:-1])
        copies = [pltpu.make_async_copy(a, b, rest[-1].at[n]) for n, (a, b) in enumerate(zip(held, sent))]
        for copy in copies:
            copy.start()
        for copy in copies:
            copy.wait()

    shapes = (
        state_shape,
        (pair_count, OBS, OBS),
        (BATCHES, ROWS, CELL_DEV),
        (BATCHES + 1, ROWS, OBS),
        square,
        square,
        square,
        square,
        square,
        (8, OBS),
    )
    known = pl.pallas_call(
        index_run,
        name="index_kernel",
        out_shape=tuple(jax.ShapeDtypeStruct(shape, f32) for shape in shapes),
        in_specs=[whole(pltpu.SMEM)] * 2 + [whole(pltpu.VMEM)] * 3 + [whole(pl.ANY)],
        out_specs=tuple(whole(pltpu.HBM) for shape in shapes[:-1]) + (whole(pltpu.VMEM),),
        scratch_shapes=[pltpu.VMEM(shape, f32) for shape in shapes[:-1]]
        + [
            pltpu.VMEM(raw_shape, f32),
            pltpu.VMEM((OBS, OBS), f32),
            pltpu.VMEM((OBS, OBS), f32),
            pltpu.VMEM((3, 16, OBS), f32),
            pltpu.VMEM(square, f32),
            pltpu.VMEM(square, f32),
            pltpu.SemaphoreType.DMA((CELL_DEV // OBS,)),
            pltpu.SemaphoreType.DMA((len(shapes) - 1,)),
        ],
        cost_estimate=pl.CostEstimate(flops=40 << 20, transcendentals=2 << 20, bytes_accessed=16 << 20),
        compiler_params=pltpu.CompilerParams(vmem_limit_bytes=62 << 20),
    )(batch_order, place, portion, table, tile_lists, flat)
    mine, token = lax.optimization_barrier((mine, known[-1]))
    known = (*known[:-1], token)
    other = lax.ppermute(mine, "lev", swap)
    mine = mine.reshape(tiles * PACK, OBS)
    other = other.reshape(tiles * PACK, OBS)

    def run(*refs):
        serial_kernel(tiles, *refs)

    result = pl.pallas_call(
        run,
        name="serial_kernel",
        out_shape=jax.ShapeDtypeStruct(flat.shape, f32),
        in_specs=[whole(pltpu.SMEM)] * 2
        + [whole(pltpu.VMEM)] * 3
        + [whole(pltpu.HBM)] * 9,
        out_specs=whole(pl.ANY),
        scratch_shapes=[pltpu.VMEM(shape, f32) for shape in shapes[:-1]]
        + [
            pltpu.VMEM(raw_shape, f32),
            pltpu.VMEM((2 * BATCHES, OBS, OBS), f32),
            pltpu.VMEM((4, OBS, OBS), bf16),
            pltpu.VMEM((1, OBS, OBS), f32),
            pltpu.SemaphoreType.DMA((CELL_DEV // OBS,)),
            pltpu.SemaphoreType.DMA((len(shapes) - 1,)),
        ],
        compiler_params=pltpu.CompilerParams(vmem_limit_bytes=60 << 20),
    )(batch_order, place, mine, other, known[-1], *known[:-1])
    return result.reshape(MEM, LEV_DEV, CELL_DEV)


def solution(mesh):
    finer = Mesh(
        mesh.devices.reshape(4, 4, 4, mesh.shape["lev"]), ("lon_0", "lon_1", "lon_2", "lev")
    )
    in_specs = (
        P(None, "lev", LON),
        P(None, LON),
        P(None, LON),
        P(None, LON),
        P(None, "lev", None),
        P(None, LON),
        P(),
    )
    out_specs = P(None, "lev", LON)
    return jax.shard_map(body, mesh=finer, in_specs=in_specs, out_specs=out_specs, check_vma=False)
```

```python
import jax
import jax.numpy as jnp
from jax import lax
from jax.experimental import pallas as pl
from jax.experimental.pallas import tpu as pltpu
from jax.sharding import Mesh
from jax.sharding import PartitionSpec as P

MEM = 80
OBS = 128
ROUTE_CAP = 24
OWN_MAX = 8
LON_DEV = 16
CELL_DEV = 1024
BATCHES = 12
LEV_DEV = 8
ROWS = 32
HALF = 6
PACK = 32
SEGMENT = 4
LAG = 3
CHUNKS = 4
WIDE = 16
LEVEL_TURNS = (2, 4, 6, 8, 10, 11, 12, 13)
LON = ("lon_0", "lon_1", "lon_2")
f32 = jnp.float32
bf16 = jnp.bfloat16


def sent_to_all(array, axis):
    copies = jnp.broadcast_to(array, (lax.axis_size(axis), *array.shape))
    return lax.all_to_all(copies, axis, split_axis=0, concat_axis=0, tiled=True)


def iota(shape, dim):
    return lax.broadcasted_iota(jnp.int32, shape, dim)


def split(x):
    high = x.astype(bf16)
    return high, (x - high.astype(f32)).astype(bf16)


def dot(a, b):
    return jnp.dot(a, b, preferred_element_type=f32)


def dot_lanes(a, b):
    return lax.dot_general(a, b, (((1,), (1,)), ((), ())), preferred_element_type=f32)


def lane_of(x, lane):
    return jnp.broadcast_to(x[:, lane : lane + 1], x.shape)


def sub_of(x, row):
    return jnp.broadcast_to(x[row : row + 1, :], x.shape)


def probe_kernel(place_ref, ens_ref, table_ref, weight_ref, keep_ref, send_ref, turn_ref, block_ref, sem):
    tile, level_half = place_ref[0], place_ref[1]
    width = CELL_DEV // CHUNKS
    fetches = [
        pltpu.make_async_copy(ens_ref.at[:, width * c : width * c + width], block_ref.at[c], sem.at[c])
        for c in range(CHUNKS)
    ]
    for fetch in fetches:
        fetch.start()
    cells = table_ref[0:16, :].astype(jnp.int32)
    own = (cells >> 10) == tile
    lane = iota((OBS, OBS), 1)
    sub = iota((OBS, OBS), 0)
    before = (sub < lane).astype(f32).astype(bf16)
    rank = dot(own.astype(f32).astype(bf16), before)
    slot = jnp.where(own, iota((16, OBS), 0).astype(f32) * OWN_MAX + rank, -1.0)
    turn_ref[...] = jnp.zeros((OBS, OBS), f32)
    turn_ref[0:16, :] = slot
    slot_turned = turn_ref[...].T
    within = cells & (CELL_DEV - 1)
    row = (within >> 4).astype(f32)
    col = (within & 15).astype(f32)
    lane_f = lane.astype(f32)
    sub8 = iota((8, OBS), 0)
    picked = jnp.zeros((32, OBS), f32)
    for b in range(BATCHES):
        chosen = (lane_of(slot_turned, b) == lane_f).astype(f32).astype(bf16)
        weight = weight_ref[b]
        w_high = weight.astype(bf16).astype(f32)
        w_rest = weight - w_high
        w_mid = w_rest.astype(bf16).astype(f32)
        place = jnp.where(
            sub8 == 0,
            jnp.broadcast_to(row[b : b + 1, :], (8, OBS)),
            jnp.where(sub8 == 1, jnp.broadcast_to(col[b : b + 1, :], (8, OBS)), 0.0),
        )
        left = jnp.concatenate([place, w_high, w_mid, w_rest - w_mid], axis=0).astype(bf16)
        picked = picked + dot(left, chosen)
    cell = picked[0:1, :] * LON_DEV + picked[1:2, :]
    weight = picked[8:16, :] + picked[16:24, :] + picked[24:32, :]
    column = iota((width, OBS), 0).astype(f32)
    taken = jnp.zeros((MEM * LEV_DEV, OBS), f32)
    for c in range(CHUNKS):
        one_hot = (column + float(width * c) == cell).astype(f32).astype(bf16)
        fetches[c].wait()
        high, low = split(block_ref[c])
        taken = taken + (dot(high, one_hot) + dot(low, one_hot))
    summed = jnp.sum(taken.reshape(MEM, LEV_DEV, OBS) * weight[None], axis=1)
    turn_ref[...] = jnp.zeros((OBS, OBS), f32)
    turn_ref[0:MEM, :] = summed
    turn_ref[...] = turn_ref[...].T
    lane6 = iota((HALF, OBS), 1)
    for half, out_ref in ((level_half, keep_ref), (1 - level_half, send_ref)):
        first = half * (HALF * OWN_MAX)
        slots = [turn_ref[pl.ds(first + s, HALF, stride=OWN_MAX), :] for s in range(OWN_MAX)]
        out_ref[...] = jnp.zeros((PACK, OBS), f32)
        tail = jnp.zeros((HALF, OBS), f32)
        for r in range(4):
            both = jnp.where(lane6 < 64, slots[r], pltpu.roll(slots[r + 4], 64, 1))
            out_ref[HALF * r : HALF * r + HALF, :] = both
        for s in range(OWN_MAX):
            tail = jnp.where((lane6 >> 4) == s, pltpu.roll(slots[s], (16 * s + 64) % OBS, 1), tail)
        out_ref[HALF * 4 : HALF * 5, :] = tail


def split3(x):
    high = x.astype(bf16)
    rest = x - high.astype(f32)
    mid = rest.astype(bf16)
    return high, mid, (rest - mid.astype(f32)).astype(bf16)


def product_of_panel(factors, rows, panel):
    above, below = panel * WIDE, OBS - (panel + 1) * WIDE

    def placed(part):
        pieces = [part]
        if above:
            pieces.insert(0, jnp.zeros((above, OBS), bf16))
        if below:
            pieces.append(jnp.zeros((below, OBS), bf16))
        return jnp.concatenate(pieces, axis=0)

    high, mid, low = (placed(part) for part in split3(rows))
    right = jnp.concatenate([high, high, high, mid, mid, low], axis=0)
    return dot(factors, right)


def added(terms):
    while len(terms) > 1:
        terms = [x + y for x, y in zip(terms[::2], terms[1::2])]
    return terms[0]


def sweep(covariance, right, root, fill):
    blocks = OBS // 8
    deep = WIDE // 8
    left_rows = [covariance[8 * i : 8 * i + 8, :] for i in range(blocks)]
    right_rows = [right[8 * i : 8 * i + 8, :] for i in range(blocks)]
    root_rows = [root[8 * i : 8 * i + 8, :] for i in range(blocks)]
    sub = iota((8, OBS), 0)
    for panel in range(OBS // WIDE):
        own = range(deep * panel, deep * panel + deep)
        near = range(own.stop, min(own.stop + deep, blocks))
        base = WIDE * panel
        a = [left_rows[i] for i in own]
        b = [right_rows[i] for i in own]
        d = [root_rows[i] for i in own]
        columns = [[lane_of(a[h], base + r) for h in range(deep)] for r in range(WIDE)]
        high, mid, low = split3(jnp.concatenate(left_rows, axis=0))
        factors = jnp.concatenate([high, mid, low, high, mid, high], axis=1)
        scale = [jnp.ones((8, OBS), f32) for h in range(deep)]
        for j in range(WIDE):
            block, at = divmod(j, 8)
            at_j = sub == at
            pivot = sub_of(columns[j][block], at)
            if j % 2 == 0:
                inverse = 1.0 / pivot
                beside = sub_of(columns[j + 1][block], at)
                corner = sub_of(columns[j + 1][block], at + 1)
                inverse_next = pivot / (pivot * corner - beside * beside)
            else:
                inverse = inverse_next
            others = list(columns[j])
            others[block] = jnp.where(at_j, 0.0, others[block])
            factor = [other * inverse for other in others]
            if j + 1 < WIDE:
                row = sub_of(columns[j + 1][block], at)
                columns[j + 1] = [c - (o * row) * inverse for c, o in zip(columns[j + 1], others)]
            for r in range(j + 2, WIDE):
                row = sub_of(columns[r][block], at)
                columns[r] = [c - f * row for c, f in zip(columns[r], factor)]
            row = sub_of(a[block], at)
            a = [x - f * row for x, f in zip(a, factor)]
            weaker = 1.0 / (1.0 + sub_of(d[block], at) * lax.rsqrt(pivot))
            b[block] = b[block] * jnp.where(at_j, weaker, 1.0)
            row = sub_of(b[block], at)
            b = [x - f * row for x, f in zip(b, factor)]
            scale[block] = jnp.where(at_j, inverse, scale[block])
        a = [x * s for x, s in zip(a, scale)]
        b = [x * s for x, s in zip(b, scale)]
        for i in near:
            factor = [lane_of(left_rows[i], base + r) for r in range(WIDE)]
            left_rows[i] = left_rows[i] - added([factor[r] * sub_of(a[r // 8], r % 8) for r in range(WIDE)])
            right_rows[i] = right_rows[i] - added([factor[r] * sub_of(b[r // 8], r % 8) for r in range(WIDE)])
        far = [i for i in range(blocks) if i not in own and i not in near]
        change = product_of_panel(factors, jnp.concatenate(b, axis=0), panel)
        for i in far:
            right_rows[i] = right_rows[i] - change[8 * i : 8 * i + 8, :]
        if panel + 1 < OBS // WIDE:
            change = product_of_panel(factors, jnp.concatenate(a, axis=0), panel)
            for i in far:
                left_rows[i] = left_rows[i] - change[8 * i : 8 * i + 8, :]
        for h, i in enumerate(own):
            left_rows[i], right_rows[i] = a[h], b[h]
        for part in range(deep):
            fill(deep * panel + part)
    return jnp.concatenate(right_rows, axis=0)


def covariance_of(spread):
    high = spread.astype(bf16)
    rest = spread - high.astype(f32)
    mid = rest.astype(bf16)
    low = (rest - mid.astype(f32)).astype(bf16)
    left = jnp.concatenate([high, high, mid, high, low, mid], axis=1)
    return dot_lanes(left, jnp.concatenate([high, mid, high, low, high, mid], axis=1))


def taper(rows_a, cols_a, rows_b, cols_b, circle):
    apart = jnp.abs(cols_a - cols_b)
    apart = jnp.minimum(apart, circle - apart)
    down = rows_a - rows_b
    return jnp.exp((apart * apart + down * down) * (-2.0 / (LON_DEV * LON_DEV)))


def pair_index(k, other):
    return k * (2 * BATCHES - 1 - k) // 2 + other - k - 1


def index_kernel(
    tiles,
    order_ref,
    place_ref,
    after_ref,
    table_ref,
    lists_ref,
    ens_ref,
    state_ref,
    pair_ref,
    local_ref,
    listed_ref,
    rank_ref,
    tile_col_ref,
    value_ref,
    root_ref,
    noise_ref,
    token_ref,
    raw_ref,
    turn_ref,
    turn2_ref,
    rows_ref,
    row_ref,
    col_ref,
    sem,
):
    circle = float(LON_DEV * tiles)
    pieces = CELL_DEV // OBS
    fetches = [
        pltpu.make_async_copy(ens_ref.at[:, OBS * c : OBS * c + OBS], raw_ref.at[c], sem.at[c])
        for c in range(pieces)
    ]
    for fetch in fetches:
        fetch.start()
    token_ref[...] = jnp.zeros((8, OBS), f32)
    listed_ref[BATCHES] = jnp.zeros((ROWS, OBS), f32)
    square = (OBS, OBS)
    lane = iota(square, 1)
    sub = iota(square, 0)
    lane_f = lane.astype(f32)
    turn_ref[...] = jnp.zeros(square, f32)
    turn2_ref[...] = jnp.full(square, float(OBS), f32)
    for k in range(BATCHES):
        b = order_ref[k]
        for part in range(3):
            turn_ref[16 * part + k : 16 * part + k + 1, :] = table_ref[pl.ds(BATCHES * part + b, 1), :]
        turn2_ref[k : k + 1, 0:ROUTE_CAP] = lists_ref[pl.ds(b, 1), :].astype(f32)
    turned = turn_ref[...].T
    listed = turn2_ref[...].T
    cells = turn_ref[0:16, :].astype(jnp.int32)
    rows_ref[0] = ((cells & (CELL_DEV - 1)) >> 4).astype(f32)
    rows_ref[1] = ((cells >> 10) * LON_DEV + (cells & 15)).astype(f32)
    rows_ref[2] = (cells >> 10).astype(f32)
    ones = jnp.ones(square, f32).astype(bf16)
    first_col = (place_ref[0] * LON_DEV).astype(f32)
    here = iota((ROWS, CELL_DEV), 1)
    here_row = (here >> 4).astype(f32)
    here_col = (here & 15).astype(f32) + first_col
    for k in range(BATCHES):
        cell = lane_of(turned, k).astype(jnp.int32)
        tile_col = (cell >> 10).astype(f32)
        row_ref[k] = ((cell & (CELL_DEV - 1)) >> 4).astype(f32)
        col_ref[k] = ((cell >> 10) * LON_DEV + (cell & 15)).astype(f32)
        tile_col_ref[k] = tile_col
        same = (tile_col == rows_ref[2, k : k + 1, :]) & (lane < sub)
        rank_ref[k] = dot(same.astype(f32).astype(bf16), ones)
        value_ref[k] = lane_of(turned, 16 + k)
        noise = lane_of(turned, 32 + k)
        noise_ref[k] = jnp.where(lane == sub, noise, 0.0)
        root_ref[k] = jnp.where(lane < MEM, jnp.sqrt(noise), 0.0)
        list_col = jnp.broadcast_to(listed[0:ROWS, k : k + 1], (ROWS, OBS))
        chosen = (list_col == lane_f[0:ROWS]).astype(f32)
        listed_ref[k] = chosen
        row_of = jnp.sum(chosen * rows_ref[0, k : k + 1, :], axis=1, keepdims=True)
        col_of = jnp.sum(chosen * rows_ref[1, k : k + 1, :], axis=1, keepdims=True)
        local_ref[k] = taper(row_of, col_of, here_row, here_col, circle) * (1.0 / (MEM - 1))

    def pairs(k, carry):
        source_row = rows_ref[0, pl.ds(k, 1), :]
        source_col = rows_ref[1, pl.ds(k, 1), :]
        source_tile = rows_ref[2, pl.ds(k, 1), :]

        def pair(other, carry):
            apart = jnp.abs(tile_col_ref[other] - source_tile)
            near = (apart <= 1.0) | (apart >= float(tiles - 1))
            weight = taper(row_ref[other], col_ref[other], source_row, source_col, circle)
            pair_ref[pair_index(k, other)] = jnp.where(near, weight * (1.0 / (MEM - 1)), 0.0)
            return carry

        return lax.fori_loop(k + 1, BATCHES, pair, carry)

    lax.fori_loop(0, BATCHES, pairs, 0)
    for fetch in fetches:
        fetch.wait()
    for c in range(pieces):
        for level in range(LEV_DEV):
            state_ref[level, :, OBS * c : OBS * c + OBS] = raw_ref[c, pl.ds(level, MEM, stride=LEV_DEV), :]


def serial_kernel(
    tiles,
    order_ref,
    place_ref,
    mine_ref,
    other_ref,
    token_ref,
    state_sent,
    pair_sent,
    local_sent,
    listed_sent,
    rank_sent,
    tile_col_sent,
    value_sent,
    root_sent,
    noise_sent,
    out_ref,
    state_ref,
    pair_ref,
    local_ref,
    listed_ref,
    rank_ref,
    tile_col_ref,
    value_ref,
    root_ref,
    noise_ref,
    raw_ref,
    paug_ref,
    past_ref,
    soon_ref,
    sem,
    sent_sem,
):
    moves = (
        (tile_col_sent, tile_col_ref),
        (rank_sent, rank_ref),
        (noise_sent, noise_ref),
        (value_sent, value_ref),
        (root_sent, root_ref),
        (listed_sent, listed_ref),
        (local_sent, local_ref),
        (pair_sent, pair_ref),
        (state_sent, state_ref),
    )
    first_pair = pltpu.make_async_copy(pair_sent.at[0:1], soon_ref, sem.at[0])
    first_pair.start()
    fetches = [pltpu.make_async_copy(a, b, sent_sem.at[n]) for n, (a, b) in enumerate(moves)]
    for fetch in fetches:
        fetch.start()
    for fetch in fetches[:2]:
        fetch.wait()
    square = (OBS, OBS)
    lane = iota(square, 1)
    lane_f = lane.astype(f32)
    is_member = lane < MEM
    group = lane >> 4
    fold = (lane == 64 + (iota(square, 0) & 15)).astype(f32).astype(bf16)
    lane_t = lane_f[:, 0:tiles]
    for k in range(BATCHES):
        b = order_ref[k]
        half = b // HALF
        here = b - half * HALF
        from_mine = half == place_ref[1]
        rank = rank_ref[k].astype(jnp.int32)
        chosen = (tile_col_ref[k, :, 0:tiles] == lane_t).astype(f32).astype(bf16)
        sent = []
        for r in range(5):
            rows = pl.ds(HALF * r + here, tiles, stride=PACK)
            sent.extend(split(jnp.where(from_mine, mine_ref[rows, :], other_ref[rows, :])))
        taken = dot(chosen, jnp.concatenate(sent, axis=1))
        parts = [taken[:, OBS * c : OBS * c + OBS] for c in range(10)]
        body = parts[0] + parts[1]
        for r in range(1, 4):
            body = jnp.where((rank & 3) == r, parts[2 * r] + parts[2 * r + 1], body)
        body = jnp.where(rank >= 4, pltpu.roll(body, 64, 1), body)
        at_rank = group == rank
        tail = dot(jnp.where(at_rank, parts[8], 0.0).astype(bf16), fold)
        tail = tail + dot(jnp.where(at_rank, parts[9], 0.0).astype(bf16), fold)
        gathered = jnp.where(lane < 64, body, tail)
        gathered = jnp.where(is_member, gathered, 0.0)
        mean = jnp.sum(gathered, axis=1, keepdims=True) * (1.0 / MEM)
        mean = jnp.broadcast_to(mean, square)
        paug_ref[k] = jnp.where(is_member, gathered - mean, jnp.where(lane == MEM, mean, 0.0))
    for fetch in fetches[2:6]:
        fetch.wait()
    first_pair.wait()

    is_member_s = is_member[0:ROWS]
    lane_s = lane[0:ROWS]
    last_pair = pair_ref.shape[0] - 1
    for extra in range(BATCHES, 2 * BATCHES):
        paug_ref[extra] = jnp.zeros(square, f32)
    for part in range(4):
        past_ref[part] = jnp.zeros(square, bf16)

    def select():
        high, low, push_high, push_low = (past_ref[part] for part in range(4))
        chosen = listed_ref[BATCHES].astype(bf16)
        return dot(chosen, high), dot(chosen, low), dot(chosen, push_high) + dot(chosen, push_low)

    def operators(s_high, s_low, gain):
        moved = pltpu.roll(s_high, MEM, 1)
        first = jnp.where(is_member_s, s_high, moved)
        second = jnp.where(lane_s < 2 * MEM - OBS, moved, pltpu.roll(s_low, 2 * MEM - OBS, 1))
        left = jnp.concatenate([first, second], axis=1).astype(bf16)
        gain = jnp.where(is_member_s, gain + lane_of(gain, MEM), 0.0)
        gain_high = gain.astype(bf16).astype(f32)
        stacked = jnp.concatenate([gain_high, gain_high, gain - gain_high, jnp.zeros_like(gain)], axis=0)
        return left, stacked.T[0:MEM, :].astype(bf16)

    def crossed_level(level, before, left, part=slice(0, CELL_DEV)):
        width = part.stop - part.start
        x_high, x_low = split(state_ref[level, :, part])
        filler = jnp.zeros((16, width), bf16)
        crossed = dot(left, jnp.concatenate([x_high, x_low, x_high, filler], axis=0))
        t_high, t_low = split(crossed * local_ref[before, :, part])
        filler = jnp.zeros((ROWS, width), bf16)
        return jnp.concatenate([t_high, t_low, t_high, filler], axis=0)

    def renew_level(level, mixing, tapered):
        state_ref[level] = state_ref[level] + dot(mixing, tapered)

    def pair_weight(pair):
        return pair_ref[jnp.clip(pair, 0, last_pair)]

    def tapered_by(upcoming, high, low, weight):
        up_high, up_low = split(jnp.where(is_member, upcoming, 0.0))
        left = jnp.concatenate([up_high, up_low, up_high], axis=1)
        crossed = dot_lanes(left, jnp.concatenate([high, high, low], axis=1))
        return split(crossed * weight)

    def pushed(parts, push_high, push_low):
        t_high, t_low = parts
        left = jnp.concatenate([t_high, t_low, t_high], axis=1)
        return dot(left, jnp.concatenate([push_high, push_high, push_low], axis=0))

    def turn(k, slots):
        before = jnp.maximum(k - 1, 0)
        now = paug_ref[k]
        spread = jnp.where(is_member, now, 0.0)
        high, low = split(spread)
        old_high, old_low, old_push_high, old_push_low = (past_ref[part] for part in range(4))
        covariance = covariance_of(spread) * (1.0 / (MEM - 1)) + noise_ref[k]
        right = jnp.where(is_member, now, jnp.where(lane == MEM, value_ref[k] - now, 0.0))
        waiting = []
        made = {}

        def finish_slot(slot, other, parts):
            upcoming = paug_ref[other] + pushed(parts, old_push_high, old_push_low)
            if slot == 0:
                made["next"] = upcoming

                def taper_next():
                    made["tapered"] = tapered_by(upcoming, high, low, pair_weight(pair_index(k, other)))

                waiting.append(taper_next)
            else:
                paug_ref[other] = upcoming

        def fill(p):
            if slots is None:
                if p == 0:
                    made["next"] = paug_ref[1]
                    made["tapered"] = tapered_by(made["next"], high, low, soon_ref[0])
                return
            ready = waiting[:-LAG] if p < OBS // 8 - 1 else waiting[:]
            del waiting[: len(ready)]
            for finish in ready:
                finish()
            if p == 0:
                made["selected"] = select()
            if p == 1:
                made["operators"] = operators(*made["selected"])
            if p < slots:
                other = k + 1 + p
                parts = tapered_by(paug_ref[other], old_high, old_low, pair_weight(pair_index(k - 1, other)))
                waiting.append(lambda: finish_slot(p, other, parts))
            if p in LEVEL_TURNS:
                level = LEVEL_TURNS.index(p)
                left, mixing = made["operators"]
                tapered = crossed_level(level, before, left)
                waiting.append(lambda: renew_level(level, mixing, tapered))

        solved = sweep(covariance, right, root_ref[k], fill)
        push = jnp.where(is_member, -solved, solved)
        push_high, push_low = split(push)
        paug_ref[k + 1] = made["next"] + pushed(made["tapered"], push_high, push_low)
        for finish in waiting:
            finish()
        for part, value in enumerate((high, low, push_high, push_low)):
            past_ref[part] = value
        listed_ref[BATCHES] = listed_ref[k]

    turn(0, None)
    for fetch in fetches[6:]:
        fetch.wait()
    for start in range(0, BATCHES, SEGMENT):
        begin = max(start, 1)

        def step(k, carry):
            turn(k, BATCHES - 1 - begin)
            return carry

        lax.fori_loop(begin, start + SEGMENT, step, 0)
    left, mixing = operators(*select())
    pieces = CELL_DEV // OBS
    stores = [
        pltpu.make_async_copy(raw_ref.at[c], out_ref.at[:, OBS * c : OBS * c + OBS], sem.at[c])
        for c in range(pieces)
    ]
    for c in range(0, pieces, 2):
        part = slice(OBS * c, OBS * c + 2 * OBS)
        tapered = [crossed_level(level, BATCHES - 1, left, part) for level in range(LEV_DEV)]
        for level in range(LEV_DEV):
            block = state_ref[level, :, part] + dot(mixing, tapered[level])
            rows = pl.ds(level, MEM, stride=LEV_DEV)
            raw_ref[c, rows, :] = block[:, 0:OBS]
            raw_ref[c + 1, rows, :] = block[:, OBS : 2 * OBS]
        stores[c].start()
        stores[c + 1].start()
    for store in stores:
        store.wait()


def whole(space):
    return pl.BlockSpec(memory_space=space)


def body(ensemble, obs_cell, obs_value, obs_noise, obs_weight, tile_lists, batch_order):
    tiles = lax.axis_size(LON)
    place = jnp.stack([lax.axis_index(LON), lax.axis_index("lev")]).astype(jnp.int32)
    mine = jnp.concatenate([obs_cell.astype(f32), obs_value, obs_noise], axis=0)
    table = sent_to_all(mine, LON)
    table = jnp.moveaxis(table, 0, 1).reshape(3 * BATCHES, OBS)
    flat = ensemble.reshape(MEM * LEV_DEV, CELL_DEV)
    packed = jax.ShapeDtypeStruct((PACK, OBS), f32)
    keep, send = pl.pallas_call(
        probe_kernel,
        name="probe_kernel",
        out_shape=(packed, packed),
        in_specs=[whole(pltpu.SMEM), whole(pl.ANY), whole(pltpu.VMEM), whole(pltpu.VMEM)],
        out_specs=(whole(pltpu.VMEM), whole(pltpu.VMEM)),
        scratch_shapes=[
            pltpu.VMEM((OBS, OBS), f32),
            pltpu.VMEM((CHUNKS, MEM * LEV_DEV, CELL_DEV // CHUNKS), f32),
            pltpu.SemaphoreType.DMA((CHUNKS,)),
        ],
        compiler_params=pltpu.CompilerParams(vmem_limit_bytes=62 << 20),
    )(place, flat, table, obs_weight)
    swap = [(0, 1), (1, 0)]
    portion = keep + lax.ppermute(send, "lev", swap)
    mine = sent_to_all(portion, LON)
    square = (BATCHES, OBS, OBS)
    pair_count = BATCHES * (BATCHES - 1) // 2
    state_shape = (LEV_DEV, MEM, CELL_DEV)
    raw_shape = (CELL_DEV // OBS, MEM * LEV_DEV, OBS)

    def index_run(*refs):
        given, sent, token, held, rest = refs[:6], refs[6:15], refs[15], refs[16:25], refs[25:]
        index_kernel(tiles, *given, *held, token, *rest[:-1])
        copies = [pltpu.make_async_copy(a, b, rest[-1].at[n]) for n, (a, b) in enumerate(zip(held, sent))]
        for copy in copies:
            copy.start()
        for copy in copies:
            copy.wait()

    shapes = (
        state_shape,
        (pair_count, OBS, OBS),
        (BATCHES, ROWS, CELL_DEV),
        (BATCHES + 1, ROWS, OBS),
        square,
        square,
        square,
        square,
        square,
        (8, OBS),
    )
    known = pl.pallas_call(
        index_run,
        name="index_kernel",
        out_shape=tuple(jax.ShapeDtypeStruct(shape, f32) for shape in shapes),
        in_specs=[whole(pltpu.SMEM)] * 2 + [whole(pltpu.VMEM)] * 3 + [whole(pl.ANY)],
        out_specs=tuple(whole(pltpu.HBM) for shape in shapes[:-1]) + (whole(pltpu.VMEM),),
        scratch_shapes=[pltpu.VMEM(shape, f32) for shape in shapes[:-1]]
        + [
            pltpu.VMEM(raw_shape, f32),
            pltpu.VMEM((OBS, OBS), f32),
            pltpu.VMEM((OBS, OBS), f32),
            pltpu.VMEM((3, 16, OBS), f32),
            pltpu.VMEM(square, f32),
            pltpu.VMEM(square, f32),
            pltpu.SemaphoreType.DMA((CELL_DEV // OBS,)),
            pltpu.SemaphoreType.DMA((len(shapes) - 1,)),
        ],
        cost_estimate=pl.CostEstimate(flops=40 << 20, transcendentals=2 << 20, bytes_accessed=16 << 20),
        compiler_params=pltpu.CompilerParams(vmem_limit_bytes=62 << 20),
    )(batch_order, place, portion, table, tile_lists, flat)
    mine, token = lax.optimization_barrier((mine, known[-1]))
    known = (*known[:-1], token)
    other = lax.ppermute(mine, "lev", swap)
    mine = mine.reshape(tiles * PACK, OBS)
    other = other.reshape(tiles * PACK, OBS)

    def run(*refs):
        serial_kernel(tiles, *refs)

    result = pl.pallas_call(
        run,
        name="serial_kernel",
        out_shape=jax.ShapeDtypeStruct(flat.shape, f32),
        in_specs=[whole(pltpu.SMEM)] * 2
        + [whole(pltpu.VMEM)] * 3
        + [whole(pltpu.HBM)] * 9,
        out_specs=whole(pl.ANY),
        scratch_shapes=[pltpu.VMEM(shape, f32) for shape in shapes[:-1]]
        + [
            pltpu.VMEM(raw_shape, f32),
            pltpu.VMEM((2 * BATCHES, OBS, OBS), f32),
            pltpu.VMEM((4, OBS, OBS), bf16),
            pltpu.VMEM((1, OBS, OBS), f32),
            pltpu.SemaphoreType.DMA((CELL_DEV // OBS,)),
            pltpu.SemaphoreType.DMA((len(shapes) - 1,)),
        ],
        compiler_params=pltpu.CompilerParams(vmem_limit_bytes=60 << 20),
    )(batch_order, place, mine, other, known[-1], *known[:-1])
    return result.reshape(MEM, LEV_DEV, CELL_DEV)


def solution(mesh):
    finer = Mesh(
        mesh.devices.reshape(4, 4, 4, mesh.shape["lev"]), ("lon_0", "lon_1", "lon_2", "lev")
    )
    in_specs = (
        P(None, "lev", LON),
        P(None, LON),
        P(None, LON),
        P(None, LON),
        P(None, "lev", None),
        P(None, LON),
        P(),
    )
    out_specs = P(None, "lev", LON)
    return jax.shard_map(body, mesh=finer, in_specs=in_specs, out_specs=out_specs, check_vma=False)
```
